512 devices in a mesh: dp: 16 (over z), segment: 2 (over y_hi), tensor: 16 (over x, y_lo, core).
Axes of the slice: x: 4, y: 4 (y_hi: 2, y_lo: 2; y = y_hi * 2 + y_lo), z: 16, core: 2. Of those that a mesh axis runs over, the one named last changes fastest.
Arguments:
- context: bfloat16 [1152, 4096], P(None, 'tensor'), may hold values from -6 to 6
- residual: bfloat16 [1152, 4096], P(None, 'dp'), may hold values from -6 to 6
- inverse_rms: float32 [1152], replicated, may hold values from 0.5 to 2
- norm_gain: float32 [4096], P('dp'), may hold values from 0.5 to 1.5
- gate_preact: bfloat16 [1152, 14336], P(None, 'tensor'), may hold values from -6 to 6
- up_preact: bfloat16 [1152, 14336], P(None, 'tensor'), may hold values from -6 to 6
- upstream: bfloat16 [1152, 4096], P(None, 'dp'), may hold values from -6 to 6
- gate_weight: bfloat16 [4096, 14336], P('dp', 'tensor'), may hold values from -0.09375 to 0.09375
- up_weight: bfloat16 [4096, 14336], P('dp', 'tensor'), may hold values from -0.09375 to 0.09375
- down_weight: bfloat16 [14336, 4096], P('tensor', 'dp'), may hold values from -0.046875 to 0.046875
- policy_logprob: float32 [32], replicated, may hold values from -270 to -230
- ref_logprob: float32 [32], replicated, may hold values from -270 to -230
- lengths: int32 [32], replicated, may hold values from 4061 to 4096
Outputs:
- residual_grad: bfloat16 [1152, 4096], P('tensor', 'dp')
- output_weight_grad: bfloat16 [4096, 4096], P('tensor', ('dp', 'segment'))
- gate_weight_grad: bfloat16 [4096, 14336], P(('dp', 'segment'), 'tensor')
- up_weight_grad: bfloat16 [4096, 14336], P(('dp', 'segment'), 'tensor')
- down_weight_grad: bfloat16 [14336, 4096], P('tensor', ('dp', 'segment'))
The draws below stay inside these ranges and needn't reach their ends.
Inputs may be any that keep to these rules, and one draw needn't show every extreme that they name: `lengths`: the window holds positions 4060 to 4095 of every sequence; a position counts where it is below the sequence's length.
All inputs are finite; a program needn't handle non-finite values.
Results may differ from the reference program's by a relative error of at most 0.03.
Values may be sent and summed in bfloat16 or wider, within the bound.
A program may use at most 64 MiB of HBM per device.

```python
import math
import jax
import jax.numpy as jnp
from jax import lax

D = 4096
FF = 14336
POS = 36
LEN = 4096
CTX_W = 4096
SEQS = 32
TOK = 1152
FEAT_DEV = 256
N_DP = 16


def with_ends(entries, key, smallest, largest):
    longest = entries.shape.index(max(entries.shape))
    spots = []
    for shift in (0, 1):
        where = [jax.random.randint(jax.random.fold_in(key, axis), (), 0, length) for axis, length in enumerate(entries.shape)]
        where[longest] = (where[longest] + shift) % entries.shape[longest]
        spots.append(tuple(where))
    return entries.at[spots[0]].set(smallest).at[spots[1]].set(largest)


def levels(own_key, extent, shards, low, high):
    def one(dim, blocks):
        draws = jax.random.uniform(jax.random.fold_in(jax.random.fold_in(own_key, 6), dim), (blocks,), jnp.float32, low / len(shards), high / len(shards))
        return jnp.repeat(jnp.exp(draws), extent[dim] // blocks).reshape((-1,) + (1,) * (len(extent) - dim - 1))

    level = one(*shards[0])
    for cut in shards[1:]:
        level = level * one(*cut)
    return level


def gaussian(key, shape, width, reach, shards=(), kind=jnp.bfloat16):
    loudness = levels(key, shape, shards, -0.22, 0.18) if shards else 1.0
    result = jax.random.normal(key, shape, jnp.float32) * width * loudness
    return jnp.minimum(jnp.maximum(result, -reach), reach).astype(kind)


def setup_inputs(seed: int = 0) -> dict:
    seeds = jax.random.split(jax.random.key(seed), 14)
    return {
        "context": gaussian(seeds[0], (TOK, CTX_W), 1.0, 6.0, ((1, 16),)),
        "residual": gaussian(seeds[1], (TOK, D), 1.0, 6.0, ((1, 16),)),
        "inverse_rms": jnp.clip(jnp.exp(jax.random.uniform(seeds[2], (TOK,), jnp.float32, math.log(0.5), math.log(2.0))), 0.5, 2.0),
        "norm_gain": jnp.clip(1.0 + 0.1 * jax.random.normal(seeds[3], (D,), jnp.float32), 0.5, 1.5),
        "gate_preact": gaussian(seeds[4], (TOK, FF), 1.0, 6.0, ((1, 16),)),
        "up_preact": gaussian(seeds[5], (TOK, FF), 1.0, 6.0, ((1, 16),)),
        "upstream": gaussian(seeds[6], (TOK, D), 0.5, 6.0, ((1, 16),)),
        "gate_weight": gaussian(seeds[7], (D, FF), D ** -0.5, 0.09375, ((0, 16), (1, 16))),
        "up_weight": gaussian(seeds[8], (D, FF), D ** -0.5, 0.09375, ((0, 16), (1, 16))),
        "down_weight": gaussian(seeds[9], (FF, D), FF ** -0.5, 0.046875, ((0, 16), (1, 16))),
        "policy_logprob": jnp.clip(jax.random.uniform(seeds[10], (SEQS,), jnp.float32, -270.0, -230.0), -270.0, -230.0),
        "ref_logprob": jnp.clip(jax.random.uniform(seeds[11], (SEQS,), jnp.float32, -270.0, -230.0), -270.0, -230.0),
        "lengths": with_ends(jax.random.randint(seeds[12], (SEQS,), LEN - POS + 1, LEN + 1), jax.random.fold_in(seeds[12], 1), LEN - POS + 1, LEN).astype(jnp.int32),
    }


def reference(context, residual, inverse_rms, norm_gain, gate_preact, up_preact, upstream, gate_weight, up_weight, down_weight, policy_logprob, ref_logprob, lengths):
    npo_weight = 2.0 * jax.nn.sigmoid(0.1 * (policy_logprob - ref_logprob))
    positions = jnp.arange(TOK, dtype=jnp.int32)
    sequence_of = positions // POS
    position_in = LEN - POS + positions % POS
    token_weight = jnp.where(position_in < lengths[sequence_of], npo_weight[sequence_of], 0.0)
    weighted = (upstream.astype(jnp.float32) * token_weight[:, None]).astype(jnp.bfloat16)
    residual_value = residual.astype(jnp.float32)
    normed = (residual_value * inverse_rms[:, None] * norm_gain[None, :]).astype(jnp.bfloat16)
    gate_value = gate_preact.astype(jnp.float32)
    up_value = up_preact.astype(jnp.float32)
    squash = jax.nn.sigmoid(gate_value)
    hidden = (gate_value * squash * up_value).astype(jnp.bfloat16)
    down_weight_grad = jnp.dot(hidden.T, weighted, preferred_element_type=jnp.float32).astype(jnp.bfloat16)
    hidden_delta = jnp.zeros((TOK, FF), jnp.float32)
    for block_index in range(N_DP):
        block_start = block_index * FEAT_DEV
        partial_sum = jnp.dot(weighted[:, block_start:block_start + FEAT_DEV], down_weight[:, block_start:block_start + FEAT_DEV].T, preferred_element_type=jnp.float32)
        rounded = lax.optimization_barrier(partial_sum.astype(jnp.bfloat16))
        hidden_delta = hidden_delta + rounded.astype(jnp.float32)
    gate_delta = (hidden_delta * up_value * squash * (1.0 + gate_value * (1.0 - squash))).astype(jnp.bfloat16)
    up_delta = (hidden_delta * gate_value * squash).astype(jnp.bfloat16)
    gate_weight_grad = jnp.dot(normed.T, gate_delta, preferred_element_type=jnp.float32).astype(jnp.bfloat16)
    up_weight_grad = jnp.dot(normed.T, up_delta, preferred_element_type=jnp.float32).astype(jnp.bfloat16)
    normed_delta = jnp.dot(gate_delta, gate_weight.T, preferred_element_type=jnp.float32) + jnp.dot(up_delta, up_weight.T, preferred_element_type=jnp.float32)
    row_dot = jnp.sum(norm_gain[None, :] * normed_delta * residual_value, axis=1)
    row_scale = inverse_rms * inverse_rms * inverse_rms * row_dot / D
    residual_grad = (weighted.astype(jnp.float32) + inverse_rms[:, None] * norm_gain[None, :] * normed_delta - residual_value * row_scale[:, None]).astype(jnp.bfloat16)
    output_weight_grad = jnp.dot(context.T, residual_grad, preferred_element_type=jnp.float32).astype(jnp.bfloat16)
    return residual_grad, output_weight_grad, gate_weight_grad, up_weight_grad, down_weight_grad
```

```python
import functools
import math

import jax
import jax.numpy as jnp
from jax import lax
from jax.experimental import pallas as pl
from jax.experimental.pallas import tpu as pltpu
from jax.sharding import PartitionSpec as P

POS = 36
LEN = 4096
PIECES = 4
MESH = pl.DeviceIdType.MESH
BF16 = jnp.bfloat16
F32 = jnp.float32


def wrapped(value, count):
    return lax.rem(value + count, count)


def dot_nt(a, b):
    return lax.dot_general(a, b, (((1,), (1,)), ((), ())), preferred_element_type=F32)


def dot_tn(a, b):
    return lax.dot_general(a, b, (((0,), (0,)), ((), ())), preferred_element_type=F32)


def kernel(
    size,
    context_hbm,
    residual_hbm,
    rms_row,
    gain_row,
    gate_hbm,
    up_hbm,
    upstream_hbm,
    gate_weight_hbm,
    up_weight_hbm,
    down_weight_hbm,
    policy_row,
    ref_row,
    lengths_row,
    residual_grad,
    output_grad,
    gate_grad,
    up_grad,
    down_grad,
    context,
    residual,
    gate,
    up,
    upstream,
    gate_weight,
    up_weight,
    down_weight,
    weighted,
    normed,
    rms,
    partial,
    came_down,
    came_up,
    delta,
    gate_factor,
    up_factor,
    gate_delta,
    up_delta,
    down_total,
    row_products,
    share_out,
    share_in,
    normed_delta,
    other_half,
    dot_z,
    dot_plane,
    dot_column,
    grads,
    grad_groups,
    weight_out,
    weight_in,
    weight_own,
    load_sem,
    sum_sems,
    gather_sems,
    share_sems,
    spread_sems,
    other_sems,
    z_sems,
    plane_sems,
    weight_sems,
):
    n_dp, n_tensor, rows, hidden, features = size
    half_rows = rows // 2
    lane_tiles = hidden // 128
    chunk_tiles = partial.shape[0] // n_dp
    piece = chunk_tiles // PIECES
    ring_half = n_dp // 2
    groups = n_tensor // 2
    group_rows = half_rows // groups
    pair_rows = 2 * group_rows
    half_pairs = half_rows // pair_rows
    n_plane = 2 * n_tensor

    d = lax.axis_index("dp")
    s = lax.axis_index("segment")
    t = lax.axis_index("tensor")
    me = s * n_tensor + t
    row_base = s * half_rows
    own_cols = pl.ds(pl.multiple_of(s * 128, 128), 128)
    other_cols = pl.ds(pl.multiple_of((1 - s) * 128, 128), 128)

    def row_block(start, count):
        return pl.ds(pl.multiple_of(start, 16), count)

    loads = [
        pltpu.make_async_copy(source, target, load_sem.at[index])
        for index, (source, target) in enumerate(
            (
                (upstream_hbm, upstream),
                (down_weight_hbm, down_weight),
                (gate_hbm, gate),
                (up_hbm, up),
                (residual_hbm, residual),
                (gate_weight_hbm, gate_weight),
                (up_weight_hbm, up_weight),
                (context_hbm, context),
            )
        )
    ]
    for load in loads:
        load.start()

    barrier = pltpu.get_barrier_semaphore()

    def greet_z(i, carry):
        pl.semaphore_signal(
            barrier, inc=1, device_id=(wrapped(d + i, n_dp), s, t), device_id_type=MESH
        )
        return carry

    def plane_device(i):
        peer = wrapped(me + i, n_plane)
        return (d, peer // n_tensor, lax.rem(peer, n_tensor))

    def greet_plane(i, carry):
        pl.semaphore_signal(barrier, inc=1, device_id=plane_device(i), device_id_type=MESH)
        return carry

    lax.fori_loop(1, n_dp, greet_z, 0)
    lax.fori_loop(1, n_plane, greet_plane, 0)

    npo = 2.0 * jax.nn.sigmoid(0.1 * (policy_row[...] - ref_row[...]))
    valid = lengths_row[...] - (LEN - POS)
    sequences = npo.shape[1]
    loads[0].wait()

    def weigh(i, carry):
        start = i * 144
        row = lax.broadcasted_iota(jnp.int32, (144, sequences), 0) + start
        offset = row - POS * lax.broadcasted_iota(jnp.int32, (144, sequences), 1)
        keep = (offset >= 0) & (offset < POS) & (offset < valid)
        weight = jnp.sum(jnp.where(keep, npo, 0.0), axis=1, keepdims=True)
        block = row_block(start, 144)
        weighted[block, :] = (upstream[block, :].astype(F32) * weight).astype(BF16)
        return carry

    lax.fori_loop(0, rows // 144, weigh, 0)
    loads[1].wait()

    def first_product(i, carry):
        block = weighted[row_block(row_base + 64 * i, 64), :]
        product = dot_nt(block, down_weight[...])
        for r in range(4):
            for c in range(lane_tiles):
                partial[(4 * i + r) * lane_tiles + c] = product[
                    16 * r : 16 * r + 16, 128 * c : 128 * c + 128
                ].astype(BF16)
        return carry

    lax.fori_loop(0, half_rows // 64, first_product, 0)
    for tile in range(half_rows // 16 * lane_tiles, partial.shape[0]):
        partial[tile] = jnp.zeros((16, 128), BF16)

    def factor_block(i):
        block = row_block(i * 144, 144)
        source = row_block(row_base + i * 144, 144)
        gate_value = gate[source, :].astype(F32)
        up_value = up[source, :].astype(F32)
        squash = jax.nn.sigmoid(gate_value)
        gate_factor[block, :] = up_value * squash * (1.0 + gate_value * (1.0 - squash))
        up_factor[block, :] = gate_value * squash

    def hidden_block(i):
        block = row_block(i * 144, 144)
        gate_value = gate[block, :].astype(F32)
        up_value = up[block, :].astype(F32)
        value = (gate_value * jax.nn.sigmoid(gate_value) * up_value).astype(BF16)
        down_total[...] += dot_tn(value, weighted[block, own_cols])

    def norm_block(i):
        block = row_block(i * 128, 128)
        column = jnp.transpose(
            jnp.broadcast_to(rms_row[:, pl.ds(pl.multiple_of(i * 128, 128), 128)], (128, 128))
        )
        rms[block, :] = column
        for c in range(features // 128):
            cols = slice(128 * c, 128 * c + 128)
            normed[block, cols] = (
                residual[block, cols].astype(F32) * column * gain_row[:, cols]
            ).astype(BF16)

    down_total[...] = jnp.zeros(down_total.shape, F32)

    pl.semaphore_wait(barrier, n_dp - 1 + n_plane - 1)

    above = (wrapped(d + 1, n_dp), s, t)
    below = (wrapped(d - 1, n_dp), s, t)

    def tiles_of(chunk, p):
        return pl.ds(chunk * chunk_tiles + p * piece, piece)

    def sum_copy(source, buffer, way, j, p, target):
        return pltpu.make_async_remote_copy(
            src_ref=source,
            dst_ref=buffer.at[j, pl.ds(p * piece, piece)],
            send_sem=sum_sems.at[way, 0, j, p],
            recv_sem=sum_sems.at[way, 1, j, p],
            device_id=target,
            device_id_type=MESH,
        )

    def down_chunk(j):
        return wrapped(d - ring_half + j, n_dp)

    def up_chunk(j):
        return wrapped(d + ring_half - 1 - j, n_dp)

    ways = ((came_down, 0, below, down_chunk), (came_up, 1, above, up_chunk))

    def begin_sum(way, p):
        buffer, index, target, chunk_of = ways[way]
        sum_copy(partial.at[tiles_of(chunk_of(0), p)], buffer, index, 0, p, target).start()

    def step_sum(way, j, p):
        buffer, index, target, chunk_of = ways[way]
        here = pl.ds(p * piece, piece)
        held = buffer.at[j - 1, here]
        sum_copy(held, buffer, index, j - 1, p, target).wait_recv()
        own = partial[tiles_of(chunk_of(j), p)]
        buffer[j - 1, here] = (buffer[j - 1, here].astype(F32) + own.astype(F32)).astype(BF16)
        sum_copy(held, buffer, index, j, p, target).start()

    for p in range(PIECES):
        begin_sum(0, p)
        begin_sum(1, p)
    loads[2].wait()
    loads[3].wait()
    factor_steps = half_rows // 144

    def sum_step(j, carry):
        for p in range(PIECES):
            step_sum(0, j, p)
            step_sum(1, j, p)

        @pl.when(j <= factor_steps)
        def _():
            factor_block(j - 1)

        return carry

    lax.fori_loop(1, ring_half - 1, sum_step, 0)
    for i in range(ring_half - 2, factor_steps):
        factor_block(i)
    for p in range(PIECES):
        step_sum(0, ring_half - 1, p)
    loads[4].wait()

    def gather_copy(chunk, way, j, p, target):
        tiles = tiles_of(chunk, p)
        return pltpu.make_async_remote_copy(
            src_ref=delta.at[tiles],
            dst_ref=delta.at[tiles],
            send_sem=gather_sems.at[way, 0, j, p],
            recv_sem=gather_sems.at[way, 1, j, p],
            device_id=target,
            device_id_type=MESH,
        )

    for p in range(PIECES):
        here = pl.ds(p * piece, piece)
        sum_copy(came_down.at[ring_half - 1, here], came_down, 0, ring_half - 1, p, below).wait_recv()
        sum_copy(came_up.at[ring_half - 2, here], came_up, 1, ring_half - 2, p, above).wait_recv()
        delta[tiles_of(d, p)] = (
            came_down[ring_half - 1, here].astype(F32)
            + came_up[ring_half - 2, here].astype(F32)
            + partial[tiles_of(d, p)].astype(F32)
        ).astype(BF16)
        gather_copy(d, 0, 0, p, above).start()
        gather_copy(d, 1, 0, p, below).start()

    def step_gather(way, j, p):
        if way == 0:
            chunk, target = wrapped(d - j, n_dp), above
        else:
            chunk, target = wrapped(d + j, n_dp), below
        gather_copy(chunk, way, j - 1, p, target).wait_recv()
        gather_copy(chunk, way, j, p, target).start()

    hidden_steps = rows // 144
    norm_steps = rows // 128

    def gather_step(j, carry):
        for p in range(PIECES):
            step_gather(0, j, p)
            step_gather(1, j, p)
        hidden_block(j - 1)
        norm_block(j - 1)
        return carry

    lax.fori_loop(1, ring_half - 1, gather_step, 0)
    for p in range(PIECES):
        step_gather(0, ring_half - 1, p)
    lax.fori_loop(ring_half - 2, hidden_steps, lambda i, c: (hidden_block(i), c)[1], 0)
    lax.fori_loop(ring_half - 2, norm_steps, lambda i, c: (norm_block(i), c)[1], 0)
    down_grad[...] = down_total[...].astype(BF16)
    loads[5].wait()
    loads[6].wait()
    loads[7].wait()
    for p in range(PIECES):
        gather_copy(wrapped(d - ring_half, n_dp), 0, ring_half - 1, p, above).wait_recv()
        gather_copy(wrapped(d + ring_half - 1, n_dp), 1, ring_half - 2, p, below).wait_recv()

    def gate_block(i, carry):
        block = row_block(i * 16, 16)
        value = jnp.concatenate(
            [delta[i * lane_tiles + c] for c in range(lane_tiles)], axis=1
        ).astype(F32)
        gate_delta[block, :] = (value * gate_factor[block, :]).astype(BF16)
        up_delta[block, :] = (value * up_factor[block, :]).astype(BF16)
        return carry

    lax.fori_loop(0, half_rows // 16, gate_block, 0)

    def share_copy(slot, owner, source):
        return pltpu.make_async_remote_copy(
            src_ref=share_out.at[slot],
            dst_ref=share_in.at[source],
            send_sem=share_sems.at[0, slot],
            recv_sem=share_sems.at[1, source],
            device_id=(d, s, owner),
            device_id_type=MESH,
        )

    def share_block(i, carry):
        block = row_block(i * pair_rows, pair_rows)
        source = row_block(row_base + i * pair_rows, pair_rows)
        product = dot_nt(gate_delta[block, :], gate_weight[...]) + dot_nt(
            up_delta[block, :], up_weight[...]
        )
        for q in range(2):
            for c in range(2):
                owner = 4 * i + 2 * q + c
                share_out[owner] = product[
                    q * group_rows : (q + 1) * group_rows, 128 * c : 128 * c + 128
                ].astype(BF16)

                @pl.when(owner != t)
                def _():
                    share_copy(owner, owner, t).start()

                @pl.when(owner == t)
                def _():
                    share_in[t] = share_out[t]

        scaled = product * residual[source, :].astype(F32) * gain_row[...]
        row_products[block, :] = scaled[:, :128] + scaled[:, 128:]
        return carry

    row_products[half_rows:, :] = jnp.zeros((row_products.shape[0] - half_rows, 128), F32)
    lax.fori_loop(0, half_pairs, share_block, 0)

    def z_copy(slot, peer, source):
        return pltpu.make_async_remote_copy(
            src_ref=dot_z.at[d],
            dst_ref=dot_z.at[source],
            send_sem=z_sems.at[0, slot],
            recv_sem=z_sems.at[1, source],
            device_id=(peer, s, t),
            device_id_type=MESH,
        )

    for b in range(row_products.shape[0] // 128):
        cols = slice(128 * b, 128 * b + 128)
        dot_z[d, :, cols] = jnp.sum(jnp.transpose(row_products[cols, :]), axis=0, keepdims=True)

    def send_z(i, carry):
        z_copy(i, wrapped(d + i, n_dp), d).start()
        return carry

    lax.fori_loop(1, n_dp, send_z, 0)

    own_normed_rows = row_block(row_base, half_rows)
    partner = (d, 1 - s, t)

    def weight_copy(index):
        return pltpu.make_async_remote_copy(
            src_ref=weight_out.at[index],
            dst_ref=weight_in.at[index],
            send_sem=weight_sems.at[0, index],
            recv_sem=weight_sems.at[1, index],
            device_id=partner,
            device_id_type=MESH,
        )

    weight_out[0] = dot_tn(normed[own_normed_rows, other_cols], gate_delta[...]).astype(BF16)
    weight_copy(0).start()
    weight_out[1] = dot_tn(normed[own_normed_rows, other_cols], up_delta[...]).astype(BF16)
    weight_copy(1).start()

    def wait_share(i, carry):
        source = wrapped(t + i, n_tensor)
        share_copy(source, t, source).wait_recv()
        return carry

    lax.fori_loop(1, n_tensor, wait_share, 0)
    total = share_in[0].astype(F32)
    for k in range(1, n_tensor):
        total = total + share_in[k].astype(F32)
    own_group = s * groups + t // 2
    own_half = lax.rem(t, 2)
    share_out[t] = total.astype(BF16)

    def spread_copy(slot, peer, group):
        return pltpu.make_async_remote_copy(
            src_ref=share_out.at[t],
            dst_ref=normed_delta.at[group],
            send_sem=spread_sems.at[0, slot],
            recv_sem=spread_sems.at[1, group],
            device_id=(d, own_half, peer),
            device_id_type=MESH,
        )

    other_copy = pltpu.make_async_remote_copy(
        src_ref=share_out.at[t],
        dst_ref=other_half,
        send_sem=other_sems.at[0],
        recv_sem=other_sems.at[1],
        device_id=(d, 1 - own_half, own_group),
        device_id_type=MESH,
    )
    keeps = own_half == s
    other_here = (own_half != s) & (own_group == t)

    def send_spread(i, carry):
        spread_copy(i, wrapped(t + i, n_tensor), own_group).start()
        return carry

    lax.fori_loop(1, n_tensor, send_spread, 0)

    @pl.when(keeps)
    def _():
        normed_delta[own_group] = share_out[t]

    @pl.when(jnp.logical_not(keeps))
    def _():
        spread_copy(0, t, own_group).start()

    @pl.when(other_here)
    def _():
        other_half[...] = share_out[t]

    @pl.when(jnp.logical_not(other_here))
    def _():
        other_copy.start()

    def wait_z(i, carry):
        source = wrapped(d + i, n_dp)
        z_copy(i, source, source).wait_recv()
        return carry

    lax.fori_loop(1, n_dp, wait_z, 0)
    z_total = dot_z[0]
    for k in range(1, n_dp):
        z_total = z_total + dot_z[k]
    dot_plane[me] = z_total

    def plane_copy(i, source):
        return pltpu.make_async_remote_copy(
            src_ref=dot_plane.at[me],
            dst_ref=dot_plane.at[source],
            send_sem=plane_sems.at[0, i],
            recv_sem=plane_sems.at[1, source],
            device_id=plane_device(i),
            device_id_type=MESH,
        )

    def send_plane(i, carry):
        plane_copy(i, me).start()
        return carry

    lax.fori_loop(1, n_plane, send_plane, 0)

    weight_own[0] = dot_tn(normed[own_normed_rows, own_cols], gate_delta[...])
    weight_own[1] = dot_tn(normed[own_normed_rows, own_cols], up_delta[...])

    def wait_plane(i, carry):
        plane_copy(i, wrapped(me + i, n_plane)).wait_recv()
        return carry

    lax.fori_loop(1, n_plane, wait_plane, 0)
    for side in range(2):
        line = dot_plane[side * n_tensor]
        for k in range(1, n_tensor):
            line = line + dot_plane[side * n_tensor + k]
        for b in range(row_products.shape[0] // 128):
            cols = slice(128 * b, 128 * b + 128)
            dot_column[side, cols, :] = jnp.transpose(jnp.broadcast_to(line[:, cols], (128, 128)))

    def wait_spread(group, carry):
        side = group // groups
        owner = 2 * lax.rem(group, groups) + s

        @pl.when(jnp.logical_not((side == s) & (owner == t)))
        def _():
            spread_copy(0, t, group).wait_recv()

        return carry

    lax.fori_loop(0, n_tensor, wait_spread, 0)

    scale = 1.0 / (features * n_dp)

    def finish(weighted_value, residual_value, rms_value, gain_value, delta_value, dot_value):
        row_scale = rms_value * rms_value * rms_value * dot_value * scale
        return weighted_value + rms_value * gain_value * delta_value - residual_value * row_scale

    def finish_block(i, carry):
        block = row_block(i * pair_rows, pair_rows)
        side = i // half_pairs
        local = row_block((i - side * half_pairs) * pair_rows, pair_rows)
        value = finish(
            weighted[block, own_cols].astype(F32),
            residual[block, own_cols].astype(F32),
            rms[block, :],
            gain_row[:, own_cols],
            jnp.concatenate(
                [normed_delta[2 * i].astype(F32), normed_delta[2 * i + 1].astype(F32)], axis=0
            ),
            dot_column[side, local, :],
        )
        grads[block, :] = value.astype(BF16)
        grad_groups[2 * i] = value[:group_rows].astype(BF16)
        grad_groups[2 * i + 1] = value[group_rows:].astype(BF16)
        return carry

    lax.fori_loop(0, n_tensor // 2, finish_block, 0)
    output_grad[...] = dot_tn(context[...], grads[...]).astype(BF16)
    residual_grad[:, own_cols] = grad_groups[t]

    @pl.when(jnp.logical_not((t // groups == s) & (2 * lax.rem(t, groups) + 1 - s == t)))
    def _():
        other_copy.wait_recv()

    pair = t // 2
    pair_block = row_block(pair * pair_rows, pair_rows)
    pair_side = pair // half_pairs
    pair_local = row_block((pair - pair_side * half_pairs) * pair_rows, pair_rows)

    def own_rows(value):
        return jnp.where(own_half == 0, value[:group_rows], value[group_rows:])

    residual_grad[:, other_cols] = finish(
        own_rows(weighted[pair_block, other_cols].astype(F32)),
        own_rows(residual[pair_block, other_cols].astype(F32)),
        own_rows(rms[pair_block, :]),
        gain_row[:, other_cols],
        other_half[...].astype(F32),
        own_rows(dot_column[pair_side, pair_local, :]),
    ).astype(BF16)

    for index, target in enumerate((gate_grad, up_grad)):
        weight_copy(index).wait_recv()
        target[...] = (weight_own[index] + weight_in[index].astype(F32)).astype(BF16)

    def drain_ring(j, carry):
        for p in range(PIECES):
            here = pl.ds(p * piece, piece)
            sum_copy(came_down.at[0, here], came_down, 0, j, p, below).wait_send()
            gather_copy(d, 0, j, p, above).wait_send()

            @pl.when(j < ring_half - 1)
            def _():
                sum_copy(came_up.at[0, here], came_up, 1, j, p, above).wait_send()
                gather_copy(d, 1, j, p, below).wait_send()

        return carry

    lax.fori_loop(0, ring_half, drain_ring, 0)

    def drain_z(i, carry):
        z_copy(i, wrapped(d + i, n_dp), d).wait_send()
        return carry

    lax.fori_loop(1, n_dp, drain_z, 0)

    def drain_plane(i, carry):
        plane_copy(i, me).wait_send()
        return carry

    lax.fori_loop(1, n_plane, drain_plane, 0)

    def drain_share(i, carry):
        owner = wrapped(t + i, n_tensor)
        share_copy(owner, owner, t).wait_send()
        spread_copy(i, owner, own_group).wait_send()
        return carry

    lax.fori_loop(1, n_tensor, drain_share, 0)

    @pl.when(jnp.logical_not(keeps))
    def _():
        spread_copy(0, t, own_group).wait_send()

    @pl.when(jnp.logical_not(other_here))
    def _():
        other_copy.wait_send()

    for index in range(2):
        weight_copy(index).wait_send()


def shards(
    n_dp,
    n_tensor,
    context,
    residual,
    inverse_rms,
    norm_gain,
    gate_preact,
    up_preact,
    upstream,
    gate_weight,
    up_weight,
    down_weight,
    policy_logprob,
    ref_logprob,
    lengths,
):
    rows, features = residual.shape
    hidden = gate_preact.shape[1]
    half_rows = rows // 2
    groups = n_tensor // 2
    group_rows = half_rows // groups
    tiles = half_rows // 16 * (hidden // 128)
    chunk_tiles = -(-tiles // (n_dp * PIECES)) * PIECES
    ring_half = n_dp // 2
    padded = -(-half_rows // 128) * 128
    vmem = pl.BlockSpec(memory_space=pltpu.VMEM)
    hbm = pl.BlockSpec(memory_space=pl.ANY)

    def like(array):
        return pltpu.VMEM(array.shape, array.dtype)

    dma = pltpu.SemaphoreType.DMA
    size = (n_dp, n_tensor, rows, hidden, features)
    return pl.pallas_call(
        functools.partial(kernel, size),
        out_shape=(
            jax.ShapeDtypeStruct((rows // n_tensor, features), BF16),
            jax.ShapeDtypeStruct((context.shape[1], features // 2), BF16),
            jax.ShapeDtypeStruct((features // 2, hidden), BF16),
            jax.ShapeDtypeStruct((features // 2, hidden), BF16),
            jax.ShapeDtypeStruct((hidden, features // 2), BF16),
        ),
        in_specs=[hbm, hbm, vmem, vmem, hbm, hbm, hbm, hbm, hbm, hbm, vmem, vmem, vmem],
        out_specs=(vmem,) * 5,
        scratch_shapes=[
            like(context),
            like(residual),
            like(gate_preact),
            like(up_preact),
            like(upstream),
            like(gate_weight),
            like(up_weight),
            like(down_weight),
            pltpu.VMEM((rows, features), BF16),
            pltpu.VMEM((rows, features), BF16),
            pltpu.VMEM((rows, 128), F32),
            pltpu.VMEM((n_dp * chunk_tiles, 16, 128), BF16),
            pltpu.VMEM((ring_half, chunk_tiles, 16, 128), BF16),
            pltpu.VMEM((ring_half, chunk_tiles, 16, 128), BF16),
            pltpu.VMEM((n_dp * chunk_tiles, 16, 128), BF16),
            pltpu.VMEM((half_rows, hidden), F32),
            pltpu.VMEM((half_rows, hidden), F32),
            pltpu.VMEM((half_rows, hidden), BF16),
            pltpu.VMEM((half_rows, hidden), BF16),
            pltpu.VMEM((hidden, features // 2), F32),
            pltpu.VMEM((padded, 128), F32),
            pltpu.VMEM((n_tensor, group_rows, 128), BF16),
            pltpu.VMEM((n_tensor, group_rows, 128), BF16),
            pltpu.VMEM((n_tensor, group_rows, 128), BF16),
            pltpu.VMEM((group_rows, 128), BF16),
            pltpu.VMEM((n_dp, 1, padded), F32),
            pltpu.VMEM((2 * n_tensor, 1, padded), F32),
            pltpu.VMEM((2, padded, 128), F32),
            pltpu.VMEM((rows, 128), BF16),
            pltpu.VMEM((n_tensor, group_rows, 128), BF16),
            pltpu.VMEM((2, features // 2, hidden), BF16),
            pltpu.VMEM((2, features // 2, hidden), BF16),
            pltpu.VMEM((2, features // 2, hidden), F32),
            dma((8,)),
            dma((2, 2, ring_half, PIECES)),
            dma((2, 2, ring_half, PIECES)),
            dma((2, n_tensor)),
            dma((2, n_tensor)),
            dma((2,)),
            dma((2, n_dp)),
            dma((2, 2 * n_tensor)),
            dma((2, 2)),
        ],
        compiler_params=pltpu.CompilerParams(
            collective_id=0, has_side_effects=True, vmem_limit_bytes=48 * 1024 * 1024
        ),
    )(
        context,
        residual,
        inverse_rms.reshape(1, -1),
        norm_gain.reshape(1, -1),
        gate_preact,
        up_preact,
        upstream,
        gate_weight,
        up_weight,
        down_weight,
        policy_logprob.reshape(1, -1),
        ref_logprob.reshape(1, -1),
        lengths.reshape(1, -1),
    )


def solution(mesh):
    return jax.shard_map(
        functools.partial(shards, mesh.shape["dp"], mesh.shape["tensor"]),
        mesh=mesh,
        in_specs=(
            P(None, "tensor"),
            P(None, "dp"),
            P(),
            P("dp"),
            P(None, "tensor"),
            P(None, "tensor"),
            P(None, "dp"),
            P("dp", "tensor"),
            P("dp", "tensor"),
            P("tensor", "dp"),
            P(),
            P(),
            P(),
        ),
        out_specs=(
            P("tensor", "dp"),
            P("tensor", ("dp", "segment")),
            P(("dp", "segment"), "tensor"),
            P(("dp", "segment"), "tensor"),
            P("tensor", ("dp", "segment")),
        ),
        check_vma=False,
    )
```

```python
import functools
import math

import jax
import jax.numpy as jnp
from jax import lax
from jax.experimental import pallas as pl
from jax.experimental.pallas import tpu as pltpu
from jax.sharding import PartitionSpec as P

POS = 36
LEN = 4096
PIECES = 2
HIDDEN_EARLY = 3
PLACES = (8, 7, 3, 6, 4, -8, -7, -3, -6, -4, 2, -2, 1, -1)
RELAYS = (5, -5)
MESH = pl.DeviceIdType.MESH
BF16 = jnp.bfloat16
F32 = jnp.float32


def wrapped(value, count):
    return lax.rem(value + count, count)


def relay_of(place):
    if abs(place) < 3:
        return 0
    return 5 if place > 0 else -5


def goes(place, piece):
    if abs(place) < 8:
        return True
    return (place > 0) == (piece < PIECES // 2)


def dot_nt(a, b):
    return lax.dot_general(a, b, (((1,), (1,)), ((), ())), preferred_element_type=F32)


def dot_tn(a, b):
    return lax.dot_general(a, b, (((0,), (0,)), ((), ())), preferred_element_type=F32)


def kernel(
    size,
    context_hbm,
    residual_hbm,
    rms_hbm,
    gain_row,
    gate_hbm,
    up_hbm,
    upstream_hbm,
    gate_weight_hbm,
    up_weight_hbm,
    down_weight_hbm,
    policy_row,
    ref_row,
    lengths_row,
    residual_grad,
    output_grad,
    gate_grad,
    up_grad,
    down_grad,
    context,
    residual,
    gate,
    up,
    upstream,
    gate_weight,
    up_weight,
    down_weight,
    weighted,
    normed,
    rms_row,
    rms,
    partial,
    arrived,
    relayed,
    delta,
    gate_factor,
    up_factor,
    gate_delta,
    up_delta,
    down_total,
    row_products,
    share_out,
    share_in,
    normed_delta,
    other_half,
    dot_z,
    dot_plane,
    dot_column,
    grads,
    grad_groups,
    weight_out,
    weight_in,
    weight_own,
    load_sem,
    sum_sems,
    gather_sems,
    share_sems,
    spread_sems,
    other_sems,
    z_sems,
    plane_sems,
    weight_sems,
):
    n_dp, n_tensor, rows, hidden, features = size
    half_rows = rows // 2
    lane_tiles = hidden // 128
    chunk_tiles = partial.shape[0] // n_dp
    piece = chunk_tiles // PIECES
    groups = n_tensor // 2
    group_rows = half_rows // groups
    pair_rows = 2 * group_rows
    half_pairs = half_rows // pair_rows
    n_plane = 2 * n_tensor

    d = lax.axis_index("dp")
    s = lax.axis_index("segment")
    t = lax.axis_index("tensor")
    me = s * n_tensor + t
    row_base = s * half_rows
    own_cols = pl.ds(pl.multiple_of(s * 128, 128), 128)
    other_cols = pl.ds(pl.multiple_of((1 - s) * 128, 128), 128)

    def row_block(start, count):
        return pl.ds(pl.multiple_of(start, 16), count)

    loads = [
        pltpu.make_async_copy(source, target, load_sem.at[index])
        for index, (source, target) in enumerate(
            (
                (upstream_hbm, upstream),
                (down_weight_hbm, down_weight),
                (gate_hbm, gate),
                (up_hbm, up),
                (residual_hbm, residual),
                (gate_weight_hbm, gate_weight),
                (up_weight_hbm, up_weight),
                (context_hbm, context),
                (rms_hbm, rms_row.at[0]),
            )
        )
    ]
    for load in loads:
        load.start()

    barrier = pltpu.get_barrier_semaphore()

    def greet_z(i, carry):
        pl.semaphore_signal(
            barrier, inc=1, device_id=(wrapped(d + i, n_dp), s, t), device_id_type=MESH
        )
        return carry

    def plane_device(i):
        peer = wrapped(me + i, n_plane)
        return (d, peer // n_tensor, lax.rem(peer, n_tensor))

    def greet_plane(i, carry):
        pl.semaphore_signal(barrier, inc=1, device_id=plane_device(i), device_id_type=MESH)
        return carry

    for offset in (1, 2, 3):
        greet_z(offset, 0)
        greet_z(-offset, 0)
    lax.fori_loop(1, n_plane, greet_plane, 0)

    npo = 2.0 * jax.nn.sigmoid(0.1 * (policy_row[...] - ref_row[...]))
    valid = lengths_row[...] - (LEN - POS)
    sequences = npo.shape[1]
    loads[0].wait()

    def weigh(i, carry):
        start = i * 144
        row = lax.broadcasted_iota(jnp.int32, (144, sequences), 0) + start
        offset = row - POS * lax.broadcasted_iota(jnp.int32, (144, sequences), 1)
        keep = (offset >= 0) & (offset < POS) & (offset < valid)
        weight = jnp.sum(jnp.where(keep, npo, 0.0), axis=1, keepdims=True)
        block = row_block(start, 144)
        weighted[block, :] = (upstream[block, :].astype(F32) * weight).astype(BF16)
        return carry

    lax.fori_loop(0, rows // 144, weigh, 0)
    loads[1].wait()

    def first_product(i, carry):
        block = weighted[row_block(row_base + 64 * i, 64), :]
        product = dot_nt(block, down_weight[...])
        for r in range(4):
            for c in range(lane_tiles):
                partial[(4 * i + r) * lane_tiles + c] = product[
                    16 * r : 16 * r + 16, 128 * c : 128 * c + 128
                ].astype(BF16)
        return carry

    lax.fori_loop(0, half_rows // 64, first_product, 0)
    for tile in range(half_rows // 16 * lane_tiles, partial.shape[0]):
        partial[tile] = jnp.zeros((16, 128), BF16)

    def factor_block(i):
        block = row_block(i * 144, 144)
        source = row_block(row_base + i * 144, 144)
        gate_value = gate[source, :].astype(F32)
        up_value = up[source, :].astype(F32)
        squash = jax.nn.sigmoid(gate_value)
        gate_factor[block, :] = up_value * squash * (1.0 + gate_value * (1.0 - squash))
        up_factor[block, :] = gate_value * squash

    def hidden_block(i):
        block = row_block(i * 144, 144)
        gate_value = gate[block, :].astype(F32)
        up_value = up[block, :].astype(F32)
        value = (gate_value * jax.nn.sigmoid(gate_value) * up_value).astype(BF16)
        down_total[...] += dot_tn(value, weighted[block, own_cols])

    def norm_block(i):
        block = row_block(i * 128, 128)
        column = jnp.transpose(
            jnp.broadcast_to(rms_row[:, pl.ds(pl.multiple_of(i * 128, 128), 128)], (128, 128))
        )
        rms[block, :] = column
        for c in range(features // 128):
            cols = slice(128 * c, 128 * c + 128)
            normed[block, cols] = (
                residual[block, cols].astype(F32) * column * gain_row[:, cols]
            ).astype(BF16)

    down_total[...] = jnp.zeros(down_total.shape, F32)

    pl.semaphore_wait(barrier, 6 + n_plane - 1)

    def at_z(offset):
        return (wrapped(d + offset, n_dp), s, t)

    def tiles_of(chunk, p):
        return pl.ds(chunk * chunk_tiles + p * piece, piece)

    def sum_copy(slot, p, source, target):
        return pltpu.make_async_remote_copy(
            src_ref=source,
            dst_ref=arrived.at[slot, pl.ds(p * piece, piece)],
            send_sem=sum_sems.at[0, slot, p],
            recv_sem=sum_sems.at[1, slot, p],
            device_id=target,
            device_id_type=MESH,
        )

    def own_sum_copy(slot, p):
        place = PLACES[slot]
        return sum_copy(
            slot, p, partial.at[tiles_of(wrapped(d - place, n_dp), p)], at_z(relay_of(place) - place)
        )

    def relay_sum_copy(index, p):
        held = relayed.at[index, pl.ds(p * piece, piece)]
        return sum_copy(len(PLACES) + index, p, held, at_z(-RELAYS[index]))

    def added(chunk, slots, p):
        here = pl.ds(p * piece, piece)
        value = partial[tiles_of(chunk, p)].astype(F32)
        for slot in slots:
            sum_copy(slot, p, partial.at[here], below).wait_recv()
            value = value + arrived[slot, here].astype(F32)
        return value.astype(BF16)

    below = at_z(-1)
    for p in range(PIECES):
        for slot, place in enumerate(PLACES):
            if relay_of(place) and goes(place, p):
                own_sum_copy(slot, p).start()
    for p in range(PIECES):
        for slot, place in enumerate(PLACES):
            if not relay_of(place):
                own_sum_copy(slot, p).start()
    loads[2].wait()
    loads[3].wait()
    lax.fori_loop(0, half_rows // 144, lambda i, c: (factor_block(i), c)[1], 0)
    for p in range(PIECES):
        for index, relay in enumerate(RELAYS):
            slots = [
                slot
                for slot, place in enumerate(PLACES)
                if relay_of(place) == relay and goes(place, p)
            ]
            relayed[index, pl.ds(p * piece, piece)] = added(wrapped(d - relay, n_dp), slots, p)
            relay_sum_copy(index, p).start()
    lax.fori_loop(0, HIDDEN_EARLY, lambda i, c: (hidden_block(i), c)[1], 0)

    def gather_copy(kind, chunk, p, target):
        tiles = tiles_of(chunk, p)
        return pltpu.make_async_remote_copy(
            src_ref=delta.at[tiles],
            dst_ref=delta.at[tiles],
            send_sem=gather_sems.at[0, kind, p],
            recv_sem=gather_sems.at[1, kind, p],
            device_id=target,
            device_id_type=MESH,
        )

    def source_copy(kind, p):
        step = RELAYS[kind - len(PLACES)] if kind >= len(PLACES) else PLACES[kind]
        return gather_copy(kind, d, p, at_z(step))

    def relay_copy(kind, p):
        place = PLACES[kind]
        relay = relay_of(place)
        return gather_copy(kind, wrapped(d - relay, n_dp), p, at_z(place - relay))

    near = [slot for slot, place in enumerate(PLACES) if not relay_of(place)]
    far = [len(PLACES) + index for index in range(len(RELAYS))]
    for p in range(PIECES):
        delta[tiles_of(d, p)] = added(d, near + far, p)
        for kind in far:
            source_copy(kind, p).start()
    for p in range(PIECES):
        for kind in near:
            source_copy(kind, p).start()
    loads[4].wait()
    loads[8].wait()
    lax.fori_loop(0, rows // 128, lambda i, c: (norm_block(i), c)[1], 0)
    for p in range(PIECES):
        for index, relay in enumerate(RELAYS):
            source_copy(far[index], p).wait_recv()
            for kind, place in enumerate(PLACES):
                if relay_of(place) == relay and goes(place, p):
                    relay_copy(kind, p).start()
    lax.fori_loop(HIDDEN_EARLY, rows // 144, lambda i, c: (hidden_block(i), c)[1], 0)
    down_grad[...] = down_total[...].astype(BF16)
    loads[5].wait()
    loads[6].wait()
    loads[7].wait()
    for p in range(PIECES):
        for kind, place in enumerate(PLACES):
            if goes(place, p):
                gather_copy(kind, d, p, below).wait_recv()

    def gate_block(i, carry):
        block = row_block(i * 16, 16)
        value = jnp.concatenate(
            [delta[i * lane_tiles + c] for c in range(lane_tiles)], axis=1
        ).astype(F32)
        gate_delta[block, :] = (value * gate_factor[block, :]).astype(BF16)
        up_delta[block, :] = (value * up_factor[block, :]).astype(BF16)
        return carry

    lax.fori_loop(0, half_rows // 16, gate_block, 0)

    def share_copy(slot, owner, source):
        return pltpu.make_async_remote_copy(
            src_ref=share_out.at[slot],
            dst_ref=share_in.at[source],
            send_sem=share_sems.at[0, slot],
            recv_sem=share_sems.at[1, source],
            device_id=(d, s, owner),
            device_id_type=MESH,
        )

    def share_block(i, carry):
        block = row_block(i * pair_rows, pair_rows)
        source = row_block(row_base + i * pair_rows, pair_rows)
        product = dot_nt(gate_delta[block, :], gate_weight[...]) + dot_nt(
            up_delta[block, :], up_weight[...]
        )
        for q in range(2):
            for c in range(2):
                owner = 4 * i + 2 * q + c
                share_out[owner] = product[
                    q * group_rows : (q + 1) * group_rows, 128 * c : 128 * c + 128
                ].astype(BF16)

                @pl.when(owner != t)
                def _():
                    share_copy(owner, owner, t).start()

                @pl.when(owner == t)
                def _():
                    share_in[t] = share_out[t]

        scaled = product * residual[source, :].astype(F32) * gain_row[...]
        row_products[block, :] = scaled[:, :128] + scaled[:, 128:]
        return carry

    row_products[half_rows:, :] = jnp.zeros((row_products.shape[0] - half_rows, 128), F32)
    lax.fori_loop(0, half_pairs, share_block, 0)

    def z_copy(slot, peer, source):
        return pltpu.make_async_remote_copy(
            src_ref=dot_z.at[d],
            dst_ref=dot_z.at[source],
            send_sem=z_sems.at[0, slot],
            recv_sem=z_sems.at[1, source],
            device_id=(peer, s, t),
            device_id_type=MESH,
        )

    for b in range(row_products.shape[0] // 128):
        cols = slice(128 * b, 128 * b + 128)
        dot_z[d, :, cols] = jnp.sum(jnp.transpose(row_products[cols, :]), axis=0, keepdims=True)

    def send_z(i, carry):
        z_copy(i, wrapped(d + i, n_dp), d).start()
        return carry

    lax.fori_loop(1, n_dp, send_z, 0)

    own_normed_rows = row_block(row_base, half_rows)
    partner = (d, 1 - s, t)

    def weight_copy(index):
        return pltpu.make_async_remote_copy(
            src_ref=weight_out.at[index],
            dst_ref=weight_in.at[index],
            send_sem=weight_sems.at[0, index],
            recv_sem=weight_sems.at[1, index],
            device_id=partner,
            device_id_type=MESH,
        )

    weight_out[0] = dot_tn(normed[own_normed_rows, other_cols], gate_delta[...]).astype(BF16)
    weight_copy(0).start()
    weight_out[1] = dot_tn(normed[own_normed_rows, other_cols], up_delta[...]).astype(BF16)
    weight_copy(1).start()

    def wait_share(i, carry):
        source = wrapped(t + i, n_tensor)
        share_copy(source, t, source).wait_recv()
        return carry

    lax.fori_loop(1, n_tensor, wait_share, 0)
    total = share_in[0].astype(F32)
    for k in range(1, n_tensor):
        total = total + share_in[k].astype(F32)
    own_group = s * groups + t // 2
    own_half = lax.rem(t, 2)
    share_out[t] = total.astype(BF16)

    def spread_copy(slot, peer, group):
        return pltpu.make_async_remote_copy(
            src_ref=share_out.at[t],
            dst_ref=normed_delta.at[group],
            send_sem=spread_sems.at[0, slot],
            recv_sem=spread_sems.at[1, group],
            device_id=(d, own_half, peer),
            device_id_type=MESH,
        )

    other_copy = pltpu.make_async_remote_copy(
        src_ref=share_out.at[t],
        dst_ref=other_half,
        send_sem=other_sems.at[0],
        recv_sem=other_sems.at[1],
        device_id=(d, 1 - own_half, own_group),
        device_id_type=MESH,
    )
    keeps = own_half == s
    other_here = (own_half != s) & (own_group == t)

    def send_spread(i, carry):
        spread_copy(i, wrapped(t + i, n_tensor), own_group).start()
        return carry

    lax.fori_loop(1, n_tensor, send_spread, 0)

    @pl.when(keeps)
    def _():
        normed_delta[own_group] = share_out[t]

    @pl.when(jnp.logical_not(keeps))
    def _():
        spread_copy(0, t, own_group).start()

    @pl.when(other_here)
    def _():
        other_half[...] = share_out[t]

    @pl.when(jnp.logical_not(other_here))
    def _():
        other_copy.start()

    def wait_z(i, carry):
        source = wrapped(d + i, n_dp)
        z_copy(i, source, source).wait_recv()
        return carry

    lax.fori_loop(1, n_dp, wait_z, 0)
    z_total = dot_z[0]
    for k in range(1, n_dp):
        z_total = z_total + dot_z[k]
    dot_plane[me] = z_total

    def plane_copy(i, source):
        return pltpu.make_async_remote_copy(
            src_ref=dot_plane.at[me],
            dst_ref=dot_plane.at[source],
            send_sem=plane_sems.at[0, i],
            recv_sem=plane_sems.at[1, source],
            device_id=plane_device(i),
            device_id_type=MESH,
        )

    def send_plane(i, carry):
        plane_copy(i, me).start()
        return carry

    lax.fori_loop(1, n_plane, send_plane, 0)

    weight_own[0] = dot_tn(normed[own_normed_rows, own_cols], gate_delta[...])
    weight_own[1] = dot_tn(normed[own_normed_rows, own_cols], up_delta[...])

    def wait_plane(i, carry):
        plane_copy(i, wrapped(me + i, n_plane)).wait_recv()
        return carry

    lax.fori_loop(1, n_plane, wait_plane, 0)
    for side in range(2):
        line = dot_plane[side * n_tensor]
        for k in range(1, n_tensor):
            line = line + dot_plane[side * n_tensor + k]
        for b in range(row_products.shape[0] // 128):
            cols = slice(128 * b, 128 * b + 128)
            dot_column[side, cols, :] = jnp.transpose(jnp.broadcast_to(line[:, cols], (128, 128)))

    def wait_spread(group, carry):
        side = group // groups
        owner = 2 * lax.rem(group, groups) + s

        @pl.when(jnp.logical_not((side == s) & (owner == t)))
        def _():
            spread_copy(0, t, group).wait_recv()

        return carry

    lax.fori_loop(0, n_tensor, wait_spread, 0)

    scale = 1.0 / (features * n_dp)

    def finish(weighted_value, residual_value, rms_value, gain_value, delta_value, dot_value):
        row_scale = rms_value * rms_value * rms_value * dot_value * scale
        return weighted_value + rms_value * gain_value * delta_value - residual_value * row_scale

    def finish_block(i, carry):
        block = row_block(i * pair_rows, pair_rows)
        side = i // half_pairs
        local = row_block((i - side * half_pairs) * pair_rows, pair_rows)
        value = finish(
            weighted[block, own_cols].astype(F32),
            residual[block, own_cols].astype(F32),
            rms[block, :],
            gain_row[:, own_cols],
            jnp.concatenate(
                [normed_delta[2 * i].astype(F32), normed_delta[2 * i + 1].astype(F32)], axis=0
            ),
            dot_column[side, local, :],
        )
        grads[block, :] = value.astype(BF16)
        grad_groups[2 * i] = value[:group_rows].astype(BF16)
        grad_groups[2 * i + 1] = value[group_rows:].astype(BF16)
        return carry

    lax.fori_loop(0, n_tensor // 2, finish_block, 0)
    output_grad[...] = dot_tn(context[...], grads[...]).astype(BF16)
    residual_grad[:, own_cols] = grad_groups[t]

    @pl.when(jnp.logical_not((t // groups == s) & (2 * lax.rem(t, groups) + 1 - s == t)))
    def _():
        other_copy.wait_recv()

    pair = t // 2
    pair_block = row_block(pair * pair_rows, pair_rows)
    pair_side = pair // half_pairs
    pair_local = row_block((pair - pair_side * half_pairs) * pair_rows, pair_rows)

    def own_rows(value):
        return jnp.where(own_half == 0, value[:group_rows], value[group_rows:])

    residual_grad[:, other_cols] = finish(
        own_rows(weighted[pair_block, other_cols].astype(F32)),
        own_rows(residual[pair_block, other_cols].astype(F32)),
        own_rows(rms[pair_block, :]),
        gain_row[:, other_cols],
        other_half[...].astype(F32),
        own_rows(dot_column[pair_side, pair_local, :]),
    ).astype(BF16)

    for index, target in enumerate((gate_grad, up_grad)):
        weight_copy(index).wait_recv()
        target[...] = (weight_own[index] + weight_in[index].astype(F32)).astype(BF16)

    for p in range(PIECES):
        for kind in range(len(PLACES) + len(RELAYS)):
            if kind in far or goes(PLACES[kind], p):
                sum_copy(kind, p, partial.at[tiles_of(d, p)], below).wait_send()
                gather_copy(kind, d, p, below).wait_send()

    def drain_z(i, carry):
        z_copy(i, wrapped(d + i, n_dp), d).wait_send()
        return carry

    lax.fori_loop(1, n_dp, drain_z, 0)

    def drain_plane(i, carry):
        plane_copy(i, me).wait_send()
        return carry

    lax.fori_loop(1, n_plane, drain_plane, 0)

    def drain_share(i, carry):
        owner = wrapped(t + i, n_tensor)
        share_copy(owner, owner, t).wait_send()
        spread_copy(i, owner, own_group).wait_send()
        return carry

    lax.fori_loop(1, n_tensor, drain_share, 0)

    @pl.when(jnp.logical_not(keeps))
    def _():
        spread_copy(0, t, own_group).wait_send()

    @pl.when(jnp.logical_not(other_here))
    def _():
        other_copy.wait_send()

    for index in range(2):
        weight_copy(index).wait_send()


def hand_on(*refs):
    count = len(refs) // 2
    sems = refs[-1]
    copies = [
        pltpu.make_async_copy(refs[i], refs[count + i], sems.at[i]) for i in range(count)
    ]
    for copy in copies:
        copy.start()
    for copy in copies:
        copy.wait()


def shards(
    n_dp,
    n_tensor,
    context,
    residual,
    inverse_rms,
    norm_gain,
    gate_preact,
    up_preact,
    upstream,
    gate_weight,
    up_weight,
    down_weight,
    policy_logprob,
    ref_logprob,
    lengths,
):
    rows, features = residual.shape
    hidden = gate_preact.shape[1]
    half_rows = rows // 2
    groups = n_tensor // 2
    group_rows = half_rows // groups
    tiles = half_rows // 16 * (hidden // 128)
    chunk_tiles = -(-tiles // (n_dp * PIECES)) * PIECES
    ways = len(PLACES) + len(RELAYS)
    padded = -(-half_rows // 128) * 128
    vmem = pl.BlockSpec(memory_space=pltpu.VMEM)
    hbm = pl.BlockSpec(memory_space=pl.ANY)

    def like(array):
        return pltpu.VMEM(array.shape, array.dtype)

    dma = pltpu.SemaphoreType.DMA
    size = (n_dp, n_tensor, rows, hidden, features)
    out_shape = (
            jax.ShapeDtypeStruct((rows // n_tensor, features), BF16),
            jax.ShapeDtypeStruct((context.shape[1], features // 2), BF16),
            jax.ShapeDtypeStruct((features // 2, hidden), BF16),
            jax.ShapeDtypeStruct((features // 2, hidden), BF16),
            jax.ShapeDtypeStruct((hidden, features // 2), BF16),
    )
    grads = pl.pallas_call(
        functools.partial(kernel, size),
        out_shape=out_shape,
        in_specs=[hbm, hbm, hbm, vmem, hbm, hbm, hbm, hbm, hbm, hbm, vmem, vmem, vmem],
        out_specs=(vmem,) * 5,
        scratch_shapes=[
            like(context),
            like(residual),
            like(gate_preact),
            like(up_preact),
            like(upstream),
            like(gate_weight),
            like(up_weight),
            like(down_weight),
            pltpu.VMEM((rows, features), BF16),
            pltpu.VMEM((rows, features), BF16),
            pltpu.VMEM((1, rows), F32),
            pltpu.VMEM((rows, 128), F32),
            pltpu.VMEM((n_dp * chunk_tiles, 16, 128), BF16),
            pltpu.VMEM((ways, chunk_tiles, 16, 128), BF16),
            pltpu.VMEM((len(RELAYS), chunk_tiles, 16, 128), BF16),
            pltpu.VMEM((n_dp * chunk_tiles, 16, 128), BF16),
            pltpu.VMEM((half_rows, hidden), F32),
            pltpu.VMEM((half_rows, hidden), F32),
            pltpu.VMEM((half_rows, hidden), BF16),
            pltpu.VMEM((half_rows, hidden), BF16),
            pltpu.VMEM((hidden, features // 2), F32),
            pltpu.VMEM((padded, 128), F32),
            pltpu.VMEM((n_tensor, group_rows, 128), BF16),
            pltpu.VMEM((n_tensor, group_rows, 128), BF16),
            pltpu.VMEM((n_tensor, group_rows, 128), BF16),
            pltpu.VMEM((group_rows, 128), BF16),
            pltpu.VMEM((n_dp, 1, padded), F32),
            pltpu.VMEM((2 * n_tensor, 1, padded), F32),
            pltpu.VMEM((2, padded, 128), F32),
            pltpu.VMEM((rows, 128), BF16),
            pltpu.VMEM((n_tensor, group_rows, 128), BF16),
            pltpu.VMEM((2, features // 2, hidden), BF16),
            pltpu.VMEM((2, features // 2, hidden), BF16),
            pltpu.VMEM((2, features // 2, hidden), F32),
            dma((9,)),
            dma((2, ways, PIECES)),
            dma((2, ways, PIECES)),
            dma((2, n_tensor)),
            dma((2, n_tensor)),
            dma((2,)),
            dma((2, n_dp)),
            dma((2, 2 * n_tensor)),
            dma((2, 2)),
        ],
        compiler_params=pltpu.CompilerParams(
            collective_id=0, has_side_effects=True, vmem_limit_bytes=63 * 1024 * 1024
        ),
    )(
        context,
        residual,
        inverse_rms,
        norm_gain.reshape(1, -1),
        gate_preact,
        up_preact,
        upstream,
        gate_weight,
        up_weight,
        down_weight,
        policy_logprob.reshape(1, -1),
        ref_logprob.reshape(1, -1),
        lengths.reshape(1, -1),
    )
    return pl.pallas_call(
        hand_on,
        out_shape=out_shape,
        in_specs=[hbm] * 5,
        out_specs=(hbm,) * 5,
        scratch_shapes=[dma((5,))],
    )(*grads)


def solution(mesh):
    return jax.shard_map(
        functools.partial(shards, mesh.shape["dp"], mesh.shape["tensor"]),
        mesh=mesh,
        in_specs=(
            P(None, "tensor"),
            P(None, "dp"),
            P(),
            P("dp"),
            P(None, "tensor"),
            P(None, "tensor"),
            P(None, "dp"),
            P("dp", "tensor"),
            P("dp", "tensor"),
            P("tensor", "dp"),
            P(),
            P(),
            P(),
        ),
        out_specs=(
            P("tensor", "dp"),
            P("tensor", ("dp", "segment")),
            P(("dp", "segment"), "tensor"),
            P(("dp", "segment"), "tensor"),
            P("tensor", ("dp", "segment")),
        ),
        check_vma=False,
    )
```

```python
import functools
import math

import jax
import jax.numpy as jnp
from jax import lax
from jax.experimental import pallas as pl
from jax.experimental.pallas import tpu as pltpu
from jax.sharding import PartitionSpec as P

POS = 36
LEN = 4096
PIECES = 4
PLACES = (8, -8, 7, -7, 6, -6, 5, -5, 4, -4, 3, -3, 2, -2, 1, -1)
CHAIN = (8, 6, 4, 2, 0)
MESH = pl.DeviceIdType.MESH
BF16 = jnp.bfloat16
F32 = jnp.float32


def wrapped(value, count):
    return lax.rem(value + count, count)


def inward(place):
    below = max(c for c in CHAIN if c < abs(place))
    return below if place > 0 else -below


def goes(place, piece):
    if abs(place) < 8:
        return True
    return (place > 0) == (piece < PIECES // 2)


def feeders(place, piece):
    return [q for q in PLACES if inward(q) == place and goes(q, piece)]


def dot_nt(a, b):
    return lax.dot_general(a, b, (((1,), (1,)), ((), ())), preferred_element_type=F32)


def dot_tn(a, b):
    return lax.dot_general(a, b, (((0,), (0,)), ((), ())), preferred_element_type=F32)


def kernel(
    size,
    context_hbm,
    residual_hbm,
    rms_hbm,
    gain_row,
    gate_hbm,
    up_hbm,
    upstream_hbm,
    gate_weight_hbm,
    up_weight_hbm,
    down_weight_hbm,
    policy_row,
    ref_row,
    lengths_row,
    residual_grad,
    output_grad,
    gate_grad,
    up_grad,
    down_grad,
    context,
    residual,
    gate,
    up,
    upstream,
    gate_weight,
    up_weight,
    down_weight,
    weighted,
    normed,
    rms_row,
    rms,
    partial,
    arrived,
    relayed,
    delta,
    gate_factor,
    up_factor,
    gate_delta,
    up_delta,
    down_total,
    row_products,
    share_out,
    share_in,
    normed_delta,
    other_half,
    dot_z,
    dot_plane,
    dot_column,
    grads,
    grad_groups,
    weight_out,
    weight_in,
    weight_own,
    load_sem,
    sum_sems,
    gather_sems,
    share_sems,
    spread_sems,
    other_sems,
    z_sems,
    plane_sems,
    weight_sems,
):
    n_dp, n_tensor, rows, hidden, features = size
    half_rows = rows // 2
    lane_tiles = hidden // 128
    chunk_tiles = partial.shape[0] // n_dp
    piece = chunk_tiles // PIECES
    groups = n_tensor // 2
    group_rows = half_rows // groups
    pair_rows = 2 * group_rows
    half_pairs = half_rows // pair_rows
    n_plane = 2 * n_tensor

    d = lax.axis_index("dp")
    s = lax.axis_index("segment")
    t = lax.axis_index("tensor")
    me = s * n_tensor + t
    row_base = s * half_rows
    own_cols = pl.ds(pl.multiple_of(s * 128, 128), 128)
    other_cols = pl.ds(pl.multiple_of((1 - s) * 128, 128), 128)

    def row_block(start, count):
        return pl.ds(pl.multiple_of(start, 16), count)

    loads = [
        pltpu.make_async_copy(source, target, load_sem.at[index])
        for index, (source, target) in enumerate(
            (
                (upstream_hbm, upstream),
                (down_weight_hbm, down_weight),
                (gate_hbm, gate),
                (up_hbm, up),
                (residual_hbm, residual),
                (gate_weight_hbm, gate_weight),
                (up_weight_hbm, up_weight),
                (context_hbm, context),
                (rms_hbm, rms_row.at[0]),
            )
        )
    ]
    for load in loads:
        load.start()

    barrier = pltpu.get_barrier_semaphore()

    def greet_z(i, carry):
        pl.semaphore_signal(
            barrier, inc=1, device_id=(wrapped(d + i, n_dp), s, t), device_id_type=MESH
        )
        return carry

    def plane_device(i):
        peer = wrapped(me + i, n_plane)
        return (d, peer // n_tensor, lax.rem(peer, n_tensor))

    def greet_plane(i, carry):
        pl.semaphore_signal(barrier, inc=1, device_id=plane_device(i), device_id_type=MESH)
        return carry

    for offset in (1, 2, 3):
        greet_z(offset, 0)
        greet_z(-offset, 0)
    lax.fori_loop(1, n_plane, greet_plane, 0)

    npo = 2.0 * jax.nn.sigmoid(0.1 * (policy_row[...] - ref_row[...]))
    valid = lengths_row[...] - (LEN - POS)
    sequences = npo.shape[1]
    loads[0].wait()

    def weigh(i, carry):
        start = i * 144
        row = lax.broadcasted_iota(jnp.int32, (144, sequences), 0) + start
        offset = row - POS * lax.broadcasted_iota(jnp.int32, (144, sequences), 1)
        keep = (offset >= 0) & (offset < POS) & (offset < valid)
        weight = jnp.sum(jnp.where(keep, npo, 0.0), axis=1, keepdims=True)
        block = row_block(start, 144)
        weighted[block, :] = (upstream[block, :].astype(F32) * weight).astype(BF16)
        return carry

    lax.fori_loop(0, rows // 144, weigh, 0)
    loads[1].wait()

    def first_product(i, carry):
        block = weighted[row_block(row_base + 64 * i, 64), :]
        product = dot_nt(block, down_weight[...])
        for r in range(4):
            for c in range(lane_tiles):
                partial[(4 * i + r) * lane_tiles + c] = product[
                    16 * r : 16 * r + 16, 128 * c : 128 * c + 128
                ].astype(BF16)
        return carry

    lax.fori_loop(0, half_rows // 64, first_product, 0)
    for tile in range(half_rows // 16 * lane_tiles, partial.shape[0]):
        partial[tile] = jnp.zeros((16, 128), BF16)

    def factor_block(i):
        block = row_block(i * 144, 144)
        source = row_block(row_base + i * 144, 144)
        gate_value = gate[source, :].astype(F32)
        up_value = up[source, :].astype(F32)
        squash = jax.nn.sigmoid(gate_value)
        gate_factor[block, :] = up_value * squash * (1.0 + gate_value * (1.0 - squash))
        up_factor[block, :] = gate_value * squash

    def hidden_block(i):
        block = row_block(i * 144, 144)
        gate_value = gate[block, :].astype(F32)
        up_value = up[block, :].astype(F32)
        value = (gate_value * jax.nn.sigmoid(gate_value) * up_value).astype(BF16)
        down_total[...] += dot_tn(value, weighted[block, own_cols])

    def norm_block(i):
        block = row_block(i * 128, 128)
        column = jnp.transpose(
            jnp.broadcast_to(rms_row[:, pl.ds(pl.multiple_of(i * 128, 128), 128)], (128, 128))
        )
        rms[block, :] = column
        for c in range(features // 128):
            cols = slice(128 * c, 128 * c + 128)
            normed[block, cols] = (
                residual[block, cols].astype(F32) * column * gain_row[:, cols]
            ).astype(BF16)

    down_total[...] = jnp.zeros(down_total.shape, F32)

    pl.semaphore_wait(barrier, 6 + n_plane - 1)

    def at_z(offset):
        return (wrapped(d + offset, n_dp), s, t)

    def tiles_of(chunk, p):
        return pl.ds(chunk * chunk_tiles + p * piece, piece)

    def sum_copy(place, p):
        chunk = wrapped(d - place, n_dp)
        here = pl.ds(p * piece, piece)
        slot = PLACES.index(place)
        held = relayed.at[slot, here] if feeders(place, p) else partial.at[tiles_of(chunk, p)]
        return pltpu.make_async_remote_copy(
            src_ref=held,
            dst_ref=arrived.at[slot, here],
            send_sem=sum_sems.at[0, slot, p],
            recv_sem=sum_sems.at[1, slot, p],
            device_id=at_z(inward(place) - place),
            device_id_type=MESH,
        )

    def added(place, p):
        here = pl.ds(p * piece, piece)
        value = partial[tiles_of(wrapped(d - place, n_dp), p)].astype(F32)
        for feeder in feeders(place, p):
            sum_copy(feeder, p).wait_recv()
            value = value + arrived[PLACES.index(feeder), here].astype(F32)
        return value.astype(BF16)

    for p in range(PIECES):
        for place in PLACES:
            if goes(place, p) and not feeders(place, p):
                sum_copy(place, p).start()
    loads[2].wait()
    loads[3].wait()
    links = [c for c in CHAIN if 0 < c < n_dp // 2]
    factor_steps = half_rows // 144
    for number, link in enumerate(links):
        if number < factor_steps:
            factor_block(number)
        for p in range(PIECES):
            for place in (link, -link):
                relayed[PLACES.index(place), pl.ds(p * piece, piece)] = added(place, p)
                sum_copy(place, p).start()
    for number in range(len(links), factor_steps):
        factor_block(number)

    def gather_copy(place, p):
        tiles = tiles_of(wrapped(d - inward(place), n_dp), p)
        slot = PLACES.index(place)
        return pltpu.make_async_remote_copy(
            src_ref=delta.at[tiles],
            dst_ref=delta.at[tiles],
            send_sem=gather_sems.at[0, slot, p],
            recv_sem=gather_sems.at[1, slot, p],
            device_id=at_z(place - inward(place)),
            device_id_type=MESH,
        )

    for p in range(PIECES):
        delta[tiles_of(d, p)] = added(0, p)
        for place in feeders(0, p):
            gather_copy(place, p).start()
    loads[4].wait()
    loads[8].wait()
    norm_block(0)
    hidden_steps = rows // 144
    norm_steps = rows // 128
    links = links[::-1]
    ends = [i * hidden_steps // len(links) for i in range(len(links) + 1)]
    norm_ends = [1 + i * (norm_steps - 1) // len(links) for i in range(len(links) + 1)]
    for number, link in enumerate(links):
        for p in range(PIECES):
            for place in (link, -link):
                gather_copy(place, p).wait_recv()
                for fed in feeders(place, p):
                    gather_copy(fed, p).start()
        lax.fori_loop(ends[number], ends[number + 1], lambda i, c: (hidden_block(i), c)[1], 0)
        lax.fori_loop(
            norm_ends[number], norm_ends[number + 1], lambda i, c: (norm_block(i), c)[1], 0
        )
    down_grad[...] = down_total[...].astype(BF16)
    loads[5].wait()
    loads[6].wait()
    loads[7].wait()
    for p in range(PIECES):
        for place in PLACES:
            if goes(place, p) and abs(place) not in links:
                gather_copy(place, p).wait_recv()

    def gate_block(i, carry):
        block = row_block(i * 16, 16)
        value = jnp.concatenate(
            [delta[i * lane_tiles + c] for c in range(lane_tiles)], axis=1
        ).astype(F32)
        gate_delta[block, :] = (value * gate_factor[block, :]).astype(BF16)
        up_delta[block, :] = (value * up_factor[block, :]).astype(BF16)
        return carry

    lax.fori_loop(0, half_rows // 16, gate_block, 0)

    def share_copy(slot, owner, source):
        return pltpu.make_async_remote_copy(
            src_ref=share_out.at[slot],
            dst_ref=share_in.at[source],
            send_sem=share_sems.at[0, slot],
            recv_sem=share_sems.at[1, source],
            device_id=(d, s, owner),
            device_id_type=MESH,
        )

    def share_block(i, carry):
        block = row_block(i * pair_rows, pair_rows)
        source = row_block(row_base + i * pair_rows, pair_rows)
        product = dot_nt(gate_delta[block, :], gate_weight[...]) + dot_nt(
            up_delta[block, :], up_weight[...]
        )
        for q in range(2):
            for c in range(2):
                owner = 4 * i + 2 * q + c
                share_out[owner] = product[
                    q * group_rows : (q + 1) * group_rows, 128 * c : 128 * c + 128
                ].astype(BF16)

                @pl.when(owner != t)
                def _():
                    share_copy(owner, owner, t).start()

                @pl.when(owner == t)
                def _():
                    share_in[t] = share_out[t]

        scaled = product * residual[source, :].astype(F32) * gain_row[...]
        row_products[block, :] = scaled[:, :128] + scaled[:, 128:]
        return carry

    row_products[half_rows:, :] = jnp.zeros((row_products.shape[0] - half_rows, 128), F32)
    lax.fori_loop(0, half_pairs, share_block, 0)

    def z_copy(slot, peer, source):
        return pltpu.make_async_remote_copy(
            src_ref=dot_z.at[d],
            dst_ref=dot_z.at[source],
            send_sem=z_sems.at[0, slot],
            recv_sem=z_sems.at[1, source],
            device_id=(peer, s, t),
            device_id_type=MESH,
        )

    for b in range(row_products.shape[0] // 128):
        cols = slice(128 * b, 128 * b + 128)
        dot_z[d, :, cols] = jnp.sum(jnp.transpose(row_products[cols, :]), axis=0, keepdims=True)

    def send_z(i, carry):
        z_copy(i, wrapped(d + i, n_dp), d).start()
        return carry

    lax.fori_loop(1, n_dp, send_z, 0)

    own_normed_rows = row_block(row_base, half_rows)
    partner = (d, 1 - s, t)

    def weight_copy(index):
        return pltpu.make_async_remote_copy(
            src_ref=weight_out.at[index],
            dst_ref=weight_in.at[index],
            send_sem=weight_sems.at[0, index],
            recv_sem=weight_sems.at[1, index],
            device_id=partner,
            device_id_type=MESH,
        )

    weight_out[0] = dot_tn(normed[own_normed_rows, other_cols], gate_delta[...]).astype(BF16)
    weight_copy(0).start()
    weight_out[1] = dot_tn(normed[own_normed_rows, other_cols], up_delta[...]).astype(BF16)
    weight_copy(1).start()

    def wait_share(i, carry):
        source = wrapped(t + i, n_tensor)
        share_copy(source, t, source).wait_recv()
        return carry

    lax.fori_loop(1, n_tensor, wait_share, 0)
    total = share_in[0].astype(F32)
    for k in range(1, n_tensor):
        total = total + share_in[k].astype(F32)
    own_group = s * groups + t // 2
    own_half = lax.rem(t, 2)
    share_out[t] = total.astype(BF16)

    def spread_copy(slot, peer, group):
        return pltpu.make_async_remote_copy(
            src_ref=share_out.at[t],
            dst_ref=normed_delta.at[group],
            send_sem=spread_sems.at[0, slot],
            recv_sem=spread_sems.at[1, group],
            device_id=(d, own_half, peer),
            device_id_type=MESH,
        )

    other_copy = pltpu.make_async_remote_copy(
        src_ref=share_out.at[t],
        dst_ref=other_half,
        send_sem=other_sems.at[0],
        recv_sem=other_sems.at[1],
        device_id=(d, 1 - own_half, own_group),
        device_id_type=MESH,
    )
    keeps = own_half == s
    other_here = (own_half != s) & (own_group == t)

    def send_spread(i, carry):
        spread_copy(i, wrapped(t + i, n_tensor), own_group).start()
        return carry

    lax.fori_loop(1, n_tensor, send_spread, 0)

    @pl.when(keeps)
    def _():
        normed_delta[own_group] = share_out[t]

    @pl.when(jnp.logical_not(keeps))
    def _():
        spread_copy(0, t, own_group).start()

    @pl.when(other_here)
    def _():
        other_half[...] = share_out[t]

    @pl.when(jnp.logical_not(other_here))
    def _():
        other_copy.start()

    def wait_z(i, carry):
        source = wrapped(d + i, n_dp)
        z_copy(i, source, source).wait_recv()
        return carry

    lax.fori_loop(1, n_dp, wait_z, 0)
    z_total = dot_z[0]
    for k in range(1, n_dp):
        z_total = z_total + dot_z[k]
    dot_plane[me] = z_total

    def plane_copy(i, source):
        return pltpu.make_async_remote_copy(
            src_ref=dot_plane.at[me],
            dst_ref=dot_plane.at[source],
            send_sem=plane_sems.at[0, i],
            recv_sem=plane_sems.at[1, source],
            device_id=plane_device(i),
            device_id_type=MESH,
        )

    def send_plane(i, carry):
        plane_copy(i, me).start()
        return carry

    lax.fori_loop(1, n_plane, send_plane, 0)

    weight_own[0] = dot_tn(normed[own_normed_rows, own_cols], gate_delta[...])
    weight_own[1] = dot_tn(normed[own_normed_rows, own_cols], up_delta[...])

    def wait_plane(i, carry):
        plane_copy(i, wrapped(me + i, n_plane)).wait_recv()
        return carry

    lax.fori_loop(1, n_plane, wait_plane, 0)
    for side in range(2):
        line = dot_plane[side * n_tensor]
        for k in range(1, n_tensor):
            line = line + dot_plane[side * n_tensor + k]
        for b in range(row_products.shape[0] // 128):
            cols = slice(128 * b, 128 * b + 128)
            dot_column[side, cols, :] = jnp.transpose(jnp.broadcast_to(line[:, cols], (128, 128)))

    def wait_spread(group, carry):
        side = group // groups
        owner = 2 * lax.rem(group, groups) + s

        @pl.when(jnp.logical_not((side == s) & (owner == t)))
        def _():
            spread_copy(0, t, group).wait_recv()

        return carry

    lax.fori_loop(0, n_tensor, wait_spread, 0)

    scale = 1.0 / (features * n_dp)

    def finish(weighted_value, residual_value, rms_value, gain_value, delta_value, dot_value):
        row_scale = rms_value * rms_value * rms_value * dot_value * scale
        return weighted_value + rms_value * gain_value * delta_value - residual_value * row_scale

    def finish_block(i, carry):
        block = row_block(i * pair_rows, pair_rows)
        side = i // half_pairs
        local = row_block((i - side * half_pairs) * pair_rows, pair_rows)
        value = finish(
            weighted[block, own_cols].astype(F32),
            residual[block, own_cols].astype(F32),
            rms[block, :],
            gain_row[:, own_cols],
            jnp.concatenate(
                [normed_delta[2 * i].astype(F32), normed_delta[2 * i + 1].astype(F32)], axis=0
            ),
            dot_column[side, local, :],
        )
        grads[block, :] = value.astype(BF16)
        grad_groups[2 * i] = value[:group_rows].astype(BF16)
        grad_groups[2 * i + 1] = value[group_rows:].astype(BF16)
        return carry

    lax.fori_loop(0, n_tensor // 2, finish_block, 0)
    output_grad[...] = dot_tn(context[...], grads[...]).astype(BF16)
    residual_grad[:, own_cols] = grad_groups[t]

    @pl.when(jnp.logical_not((t // groups == s) & (2 * lax.rem(t, groups) + 1 - s == t)))
    def _():
        other_copy.wait_recv()

    pair = t // 2
    pair_block = row_block(pair * pair_rows, pair_rows)
    pair_side = pair // half_pairs
    pair_local = row_block((pair - pair_side * half_pairs) * pair_rows, pair_rows)

    def own_rows(value):
        return jnp.where(own_half == 0, value[:group_rows], value[group_rows:])

    residual_grad[:, other_cols] = finish(
        own_rows(weighted[pair_block, other_cols].astype(F32)),
        own_rows(residual[pair_block, other_cols].astype(F32)),
        own_rows(rms[pair_block, :]),
        gain_row[:, other_cols],
        other_half[...].astype(F32),
        own_rows(dot_column[pair_side, pair_local, :]),
    ).astype(BF16)

    for index, target in enumerate((gate_grad, up_grad)):
        weight_copy(index).wait_recv()
        target[...] = (weight_own[index] + weight_in[index].astype(F32)).astype(BF16)

    for p in range(PIECES):
        for place in PLACES:
            if goes(place, p):
                sum_copy(place, p).wait_send()
                gather_copy(place, p).wait_send()

    def drain_z(i, carry):
        z_copy(i, wrapped(d + i, n_dp), d).wait_send()
        return carry

    lax.fori_loop(1, n_dp, drain_z, 0)

    def drain_plane(i, carry):
        plane_copy(i, me).wait_send()
        return carry

    lax.fori_loop(1, n_plane, drain_plane, 0)

    def drain_share(i, carry):
        owner = wrapped(t + i, n_tensor)
        share_copy(owner, owner, t).wait_send()
        spread_copy(i, owner, own_group).wait_send()
        return carry

    lax.fori_loop(1, n_tensor, drain_share, 0)

    @pl.when(jnp.logical_not(keeps))
    def _():
        spread_copy(0, t, own_group).wait_send()

    @pl.when(jnp.logical_not(other_here))
    def _():
        other_copy.wait_send()

    for index in range(2):
        weight_copy(index).wait_send()


def hand_on(*refs):
    count = len(refs) // 2
    for source, target in zip(refs[:count], refs[count:]):
        target[...] = source[...]


def shards(
    n_dp,
    n_tensor,
    context,
    residual,
    inverse_rms,
    norm_gain,
    gate_preact,
    up_preact,
    upstream,
    gate_weight,
    up_weight,
    down_weight,
    policy_logprob,
    ref_logprob,
    lengths,
):
    rows, features = residual.shape
    hidden = gate_preact.shape[1]
    half_rows = rows // 2
    groups = n_tensor // 2
    group_rows = half_rows // groups
    tiles = half_rows // 16 * (hidden // 128)
    chunk_tiles = -(-tiles // (n_dp * PIECES)) * PIECES
    ways = len(PLACES)
    padded = -(-half_rows // 128) * 128
    vmem = pl.BlockSpec(memory_space=pltpu.VMEM)
    hbm = pl.BlockSpec(memory_space=pl.ANY)

    def like(array):
        return pltpu.VMEM(array.shape, array.dtype)

    dma = pltpu.SemaphoreType.DMA
    size = (n_dp, n_tensor, rows, hidden, features)
    out_shape = (
            jax.ShapeDtypeStruct((rows // n_tensor, features), BF16),
            jax.ShapeDtypeStruct((context.shape[1], features // 2), BF16),
            jax.ShapeDtypeStruct((features // 2, hidden), BF16),
            jax.ShapeDtypeStruct((features // 2, hidden), BF16),
            jax.ShapeDtypeStruct((hidden, features // 2), BF16),
    )
    grads = pl.pallas_call(
        functools.partial(kernel, size),
        out_shape=out_shape,
        in_specs=[hbm, hbm, hbm, vmem, hbm, hbm, hbm, hbm, hbm, hbm, vmem, vmem, vmem],
        out_specs=(vmem,) * 5,
        scratch_shapes=[
            like(context),
            like(residual),
            like(gate_preact),
            like(up_preact),
            like(upstream),
            like(gate_weight),
            like(up_weight),
            like(down_weight),
            pltpu.VMEM((rows, features), BF16),
            pltpu.VMEM((rows, features), BF16),
            pltpu.VMEM((1, rows), F32),
            pltpu.VMEM((rows, 128), F32),
            pltpu.VMEM((n_dp * chunk_tiles, 16, 128), BF16),
            pltpu.VMEM((ways, chunk_tiles, 16, 128), BF16),
            pltpu.VMEM((ways, chunk_tiles, 16, 128), BF16),
            pltpu.VMEM((n_dp * chunk_tiles, 16, 128), BF16),
            pltpu.VMEM((half_rows, hidden), F32),
            pltpu.VMEM((half_rows, hidden), F32),
            pltpu.VMEM((half_rows, hidden), BF16),
            pltpu.VMEM((half_rows, hidden), BF16),
            pltpu.VMEM((hidden, features // 2), F32),
            pltpu.VMEM((padded, 128), F32),
            pltpu.VMEM((n_tensor, group_rows, 128), BF16),
            pltpu.VMEM((n_tensor, group_rows, 128), BF16),
            pltpu.VMEM((n_tensor, group_rows, 128), BF16),
            pltpu.VMEM((group_rows, 128), BF16),
            pltpu.VMEM((n_dp, 1, padded), F32),
            pltpu.VMEM((2 * n_tensor, 1, padded), F32),
            pltpu.VMEM((2, padded, 128), F32),
            pltpu.VMEM((rows, 128), BF16),
            pltpu.VMEM((n_tensor, group_rows, 128), BF16),
            pltpu.VMEM((2, features // 2, hidden), BF16),
            pltpu.VMEM((2, features // 2, hidden), BF16),
            pltpu.VMEM((2, features // 2, hidden), F32),
            dma((9,)),
            dma((2, ways, PIECES)),
            dma((2, ways, PIECES)),
            dma((2, n_tensor)),
            dma((2, n_tensor)),
            dma((2,)),
            dma((2, n_dp)),
            dma((2, 2 * n_tensor)),
            dma((2, 2)),
        ],
        compiler_params=pltpu.CompilerParams(
            collective_id=0, has_side_effects=True, vmem_limit_bytes=63 * 1024 * 1024
        ),
    )(
        context,
        residual,
        inverse_rms,
        norm_gain.reshape(1, -1),
        gate_preact,
        up_preact,
        upstream,
        gate_weight,
        up_weight,
        down_weight,
        policy_logprob.reshape(1, -1),
        ref_logprob.reshape(1, -1),
        lengths.reshape(1, -1),
    )
    return pl.pallas_call(
        hand_on,
        out_shape=out_shape,
        in_specs=[vmem] * 5,
        out_specs=(vmem,) * 5,
    )(*grads)


def solution(mesh):
    return jax.shard_map(
        functools.partial(shards, mesh.shape["dp"], mesh.shape["tensor"]),
        mesh=mesh,
        in_specs=(
            P(None, "tensor"),
            P(None, "dp"),
            P(),
            P("dp"),
            P(None, "tensor"),
            P(None, "tensor"),
            P(None, "dp"),
            P("dp", "tensor"),
            P("dp", "tensor"),
            P("tensor", "dp"),
            P(),
            P(),
            P(),
        ),
        out_specs=(
            P("tensor", "dp"),
            P("tensor", ("dp", "segment")),
            P(("dp", "segment"), "tensor"),
            P(("dp", "segment"), "tensor"),
            P("tensor", ("dp", "segment")),
        ),
        check_vma=False,
    )
```

```python
import functools
import math

import jax
import jax.numpy as jnp
from jax import lax
from jax.experimental import pallas as pl
from jax.experimental.pallas import tpu as pltpu
from jax.sharding import PartitionSpec as P

POS = 36
LEN = 4096
PIECES = 4
PLACES = (8, -8, 7, -7, 6, -6, 5, -5, 4, -4, 3, -3, 2, -2, 1, -1)
CHAIN = (8, 6, 4, 2, 0)
MESH = pl.DeviceIdType.MESH
BF16 = jnp.bfloat16
F32 = jnp.float32


def wrapped(value, count):
    return lax.rem(value + count, count)


def inward(place):
    below = max(c for c in CHAIN if c < abs(place))
    return below if place > 0 else -below


def goes(place, piece):
    if abs(place) < 8:
        return True
    return (place > 0) == (piece < PIECES // 2)


def feeders(place, piece):
    return [q for q in PLACES if inward(q) == place and goes(q, piece)]


def dot_nt(a, b):
    return lax.dot_general(a, b, (((1,), (1,)), ((), ())), preferred_element_type=F32)


def dot_tn(a, b):
    return lax.dot_general(a, b, (((0,), (0,)), ((), ())), preferred_element_type=F32)


def kernel(
    size,
    context_hbm,
    residual_hbm,
    rms_hbm,
    gain_row,
    gate_hbm,
    up_hbm,
    upstream_hbm,
    gate_weight_hbm,
    up_weight_hbm,
    down_weight_hbm,
    policy_row,
    ref_row,
    lengths_row,
    residual_grad,
    output_grad,
    gate_grad,
    up_grad,
    down_grad,
    context,
    residual,
    gate,
    up,
    upstream,
    gate_weight,
    up_weight,
    down_weight,
    weighted,
    normed,
    rms_row,
    rms,
    partial,
    arrived,
    relayed,
    delta,
    gate_factor,
    up_factor,
    dot_factor,
    gate_delta,
    up_delta,
    down_total,
    row_products,
    share_out,
    share_in,
    normed_delta,
    other_half,
    dot_z,
    dot_plane,
    dot_column,
    base,
    pull,
    grads,
    grad_groups,
    weight_out,
    weight_in,
    weight_own,
    load_sem,
    sum_sems,
    gather_sems,
    share_sems,
    spread_sems,
    other_sems,
    z_sems,
    plane_sems,
    weight_sems,
):
    n_dp, n_tensor, rows, hidden, features = size
    half_rows = rows // 2
    lane_tiles = hidden // 128
    chunk_tiles = partial.shape[0] // n_dp
    piece = chunk_tiles // PIECES
    groups = n_tensor // 2
    group_rows = half_rows // groups
    pair_rows = 2 * group_rows
    half_pairs = half_rows // pair_rows
    n_plane = 2 * n_tensor

    d = lax.axis_index("dp")
    s = lax.axis_index("segment")
    t = lax.axis_index("tensor")
    me = s * n_tensor + t
    row_base = s * half_rows
    own_cols = pl.ds(pl.multiple_of(s * 128, 128), 128)
    other_cols = pl.ds(pl.multiple_of((1 - s) * 128, 128), 128)

    def row_block(start, count):
        return pl.ds(pl.multiple_of(start, 16), count)

    loads = [
        pltpu.make_async_copy(source, target, load_sem.at[index])
        for index, (source, target) in enumerate(
            (
                (upstream_hbm, upstream),
                (down_weight_hbm, down_weight),
                (gate_hbm, gate),
                (up_hbm, up),
                (residual_hbm, residual),
                (gate_weight_hbm, gate_weight),
                (up_weight_hbm, up_weight),
                (context_hbm, context),
                (rms_hbm, rms_row.at[0]),
            )
        )
    ]
    for load in loads:
        load.start()

    barrier = pltpu.get_barrier_semaphore()

    def greet_z(i, carry):
        pl.semaphore_signal(
            barrier, inc=1, device_id=(wrapped(d + i, n_dp), s, t), device_id_type=MESH
        )
        return carry

    def plane_device(i):
        peer = wrapped(me + i, n_plane)
        return (d, peer // n_tensor, lax.rem(peer, n_tensor))

    def greet_plane(i, carry):
        pl.semaphore_signal(barrier, inc=1, device_id=plane_device(i), device_id_type=MESH)
        return carry

    for offset in (1, 2, 3):
        greet_z(offset, 0)
        greet_z(-offset, 0)
    lax.fori_loop(1, n_plane, greet_plane, 0)

    npo = 2.0 * jax.nn.sigmoid(0.1 * (policy_row[...] - ref_row[...]))
    valid = lengths_row[...] - (LEN - POS)
    sequences = npo.shape[1]
    loads[0].wait()

    def weigh(i, carry):
        start = i * 144
        row = lax.broadcasted_iota(jnp.int32, (144, sequences), 0) + start
        offset = row - POS * lax.broadcasted_iota(jnp.int32, (144, sequences), 1)
        keep = (offset >= 0) & (offset < POS) & (offset < valid)
        weight = jnp.sum(jnp.where(keep, npo, 0.0), axis=1, keepdims=True)
        block = row_block(start, 144)
        weighted[block, :] = (upstream[block, :].astype(F32) * weight).astype(BF16)
        return carry

    lax.fori_loop(0, rows // 144, weigh, 0)
    loads[1].wait()

    def first_product(i, carry):
        block = weighted[row_block(row_base + 64 * i, 64), :]
        product = dot_nt(block, down_weight[...])
        for r in range(4):
            for c in range(lane_tiles):
                partial[(4 * i + r) * lane_tiles + c] = product[
                    16 * r : 16 * r + 16, 128 * c : 128 * c + 128
                ].astype(BF16)
        return carry

    lax.fori_loop(0, half_rows // 64, first_product, 0)
    for tile in range(half_rows // 16 * lane_tiles, partial.shape[0]):
        partial[tile] = jnp.zeros((16, 128), BF16)

    def factor_block(i):
        block = row_block(i * 144, 144)
        source = row_block(row_base + i * 144, 144)
        gate_value = gate[source, :].astype(F32)
        up_value = up[source, :].astype(F32)
        squash = jax.nn.sigmoid(gate_value)
        gate_part = up_value * squash * (1.0 + gate_value * (1.0 - squash))
        up_part = gate_value * squash
        gate_factor[block, :] = gate_part
        up_factor[block, :] = up_part
        gained = (residual[source, :].astype(F32) * gain_row[...]).astype(BF16)
        dot_factor[block, :] = gate_part * jnp.dot(
            gained, gate_weight[...], preferred_element_type=F32
        ) + up_part * jnp.dot(gained, up_weight[...], preferred_element_type=F32)

    def hidden_block(i):
        block = row_block(i * 144, 144)
        gate_value = gate[block, :].astype(F32)
        up_value = up[block, :].astype(F32)
        value = (gate_value * jax.nn.sigmoid(gate_value) * up_value).astype(BF16)
        down_total[...] += dot_tn(value, weighted[block, own_cols])

    def norm_block(i):
        block = row_block(i * 128, 128)
        column = jnp.transpose(
            jnp.broadcast_to(rms_row[:, pl.ds(pl.multiple_of(i * 128, 128), 128)], (128, 128))
        )
        rms[block, :] = column
        for c in range(features // 128):
            cols = slice(128 * c, 128 * c + 128)
            normed[block, cols] = (
                residual[block, cols].astype(F32) * column * gain_row[:, cols]
            ).astype(BF16)

    down_total[...] = jnp.zeros(down_total.shape, F32)

    pl.semaphore_wait(barrier, 6 + n_plane - 1)

    def at_z(offset):
        return (wrapped(d + offset, n_dp), s, t)

    def tiles_of(chunk, p):
        return pl.ds(chunk * chunk_tiles + p * piece, piece)

    def sum_copy(place, p):
        chunk = wrapped(d - place, n_dp)
        here = pl.ds(p * piece, piece)
        slot = PLACES.index(place)
        held = relayed.at[slot, here] if feeders(place, p) else partial.at[tiles_of(chunk, p)]
        return pltpu.make_async_remote_copy(
            src_ref=held,
            dst_ref=arrived.at[slot, here],
            send_sem=sum_sems.at[0, slot, p],
            recv_sem=sum_sems.at[1, slot, p],
            device_id=at_z(inward(place) - place),
            device_id_type=MESH,
        )

    def added(place, p):
        here = pl.ds(p * piece, piece)
        value = partial[tiles_of(wrapped(d - place, n_dp), p)].astype(F32)
        for feeder in feeders(place, p):
            sum_copy(feeder, p).wait_recv()
            value = value + arrived[PLACES.index(feeder), here].astype(F32)
        return value.astype(BF16)

    links = [c for c in CHAIN if 0 < c < n_dp // 2]

    def join(number):
        link = (links + [0])[number] if number <= len(links) else None
        for p in range(PIECES):
            for place in PLACES:
                if abs(inward(place)) == link and goes(place, p) and not feeders(place, p):
                    sum_copy(place, p).start()

    join(0)
    join(1)
    for load in loads[2:7]:
        load.wait()
    factor_steps = half_rows // 144
    for number, link in enumerate(links):
        if number < factor_steps:
            factor_block(number)
        for p in range(PIECES):
            for place in (link, -link):
                relayed[PLACES.index(place), pl.ds(p * piece, piece)] = added(place, p)
                sum_copy(place, p).start()
        join(number + 2)
    for number in range(len(links), factor_steps):
        factor_block(number)

    def gather_copy(place, p):
        tiles = tiles_of(wrapped(d - inward(place), n_dp), p)
        slot = PLACES.index(place)
        return pltpu.make_async_remote_copy(
            src_ref=delta.at[tiles],
            dst_ref=delta.at[tiles],
            send_sem=gather_sems.at[0, slot, p],
            recv_sem=gather_sems.at[1, slot, p],
            device_id=at_z(place - inward(place)),
            device_id_type=MESH,
        )

    def gate_block(i, carry):
        block = row_block(i * 16, 16)
        value = jnp.concatenate(
            [delta[i * lane_tiles + c] for c in range(lane_tiles)], axis=1
        ).astype(F32)
        gate_delta[block, :] = (value * gate_factor[block, :]).astype(BF16)
        up_delta[block, :] = (value * up_factor[block, :]).astype(BF16)
        dots = value * dot_factor[block, :]
        row_products[block, :] = sum(
            dots[:, 128 * c : 128 * c + 128] for c in range(lane_tiles)
        )
        return carry


    def share_copy(slot, owner, source):
        return pltpu.make_async_remote_copy(
            src_ref=share_out.at[slot],
            dst_ref=share_in.at[source],
            send_sem=share_sems.at[0, slot],
            recv_sem=share_sems.at[1, source],
            device_id=(d, s, owner),
            device_id_type=MESH,
        )

    def share_block(i, carry):
        block = row_block(i * pair_rows, pair_rows)
        product = dot_nt(gate_delta[block, :], gate_weight[...]) + dot_nt(
            up_delta[block, :], up_weight[...]
        )
        for q in range(2):
            for c in range(2):
                owner = 4 * i + 2 * q + c
                share_out[owner] = product[
                    q * group_rows : (q + 1) * group_rows, 128 * c : 128 * c + 128
                ].astype(BF16)

                @pl.when(owner != t)
                def _():
                    share_copy(owner, owner, t).start()

                @pl.when(owner == t)
                def _():
                    share_in[t] = share_out[t]

        return carry

    pair_tiles = pair_rows // 16

    def token_block(i):
        lax.fori_loop(i * pair_tiles, (i + 1) * pair_tiles, gate_block, 0)
        share_block(i, 0)

    row_products[half_rows:, :] = jnp.zeros((row_products.shape[0] - half_rows, 128), F32)
    here = d // (n_dp // half_pairs)
    lean = lax.rem(d, n_dp // half_pairs)
    early = lean < n_dp // half_pairs // 2
    beside = jnp.where(early, here + half_pairs - 1, here + 1)
    across = jnp.where(early, here + 1, here + half_pairs - 1)
    arrived_places = set()

    def reach(limit):
        for p in range(PIECES):
            for place in PLACES:
                if abs(place) <= limit and goes(place, p) and (place, p) not in arrived_places:
                    arrived_places.add((place, p))
                    gather_copy(place, p).wait_recv()

    for p in range(PIECES):
        delta[tiles_of(d, p)] = added(0, p)
        for place in feeders(0, p):
            gather_copy(place, p).start()
    loads[8].wait()
    norm_block(0)
    hidden_steps = rows // 144
    norm_steps = rows // 128
    links = links[::-1]
    ends = [i * hidden_steps // len(links) for i in range(len(links) + 1)]
    norm_ends = [1 + i * (norm_steps - 1) // len(links) for i in range(len(links) + 1)]
    for number, link in enumerate(links):
        for p in range(PIECES):
            for place in (link, -link):
                arrived_places.add((place, p))
                gather_copy(place, p).wait_recv()
                for fed in feeders(place, p):
                    gather_copy(fed, p).start()
        lax.fori_loop(ends[number], ends[number + 1], lambda i, c: (hidden_block(i), c)[1], 0)
        lax.fori_loop(
            norm_ends[number], norm_ends[number + 1], lambda i, c: (norm_block(i), c)[1], 0
        )
        if link == 4:
            reach(4)
            token_block(here)
        if link == 6:
            reach(6)
            token_block(lax.rem(beside, half_pairs))
    down_grad[...] = down_total[...].astype(BF16)
    loads[7].wait()
    reach(n_dp // 2)
    token_block(lax.rem(here + 2, half_pairs))
    token_block(lax.rem(across, half_pairs))

    def z_copy(slot, peer, source):
        return pltpu.make_async_remote_copy(
            src_ref=dot_z.at[d],
            dst_ref=dot_z.at[source],
            send_sem=z_sems.at[0, slot],
            recv_sem=z_sems.at[1, source],
            device_id=(peer, s, t),
            device_id_type=MESH,
        )

    for b in range(row_products.shape[0] // 128):
        cols = slice(128 * b, 128 * b + 128)
        dot_z[d, :, cols] = jnp.sum(jnp.transpose(row_products[cols, :]), axis=0, keepdims=True)

    def send_z(i, carry):
        z_copy(i, wrapped(d + i, n_dp), d).start()
        return carry

    lax.fori_loop(1, n_dp, send_z, 0)

    own_normed_rows = row_block(row_base, half_rows)
    partner = (d, 1 - s, t)

    def weight_copy(index):
        return pltpu.make_async_remote_copy(
            src_ref=weight_out.at[index],
            dst_ref=weight_in.at[index],
            send_sem=weight_sems.at[0, index],
            recv_sem=weight_sems.at[1, index],
            device_id=partner,
            device_id_type=MESH,
        )

    weight_out[0] = dot_tn(normed[own_normed_rows, other_cols], gate_delta[...]).astype(BF16)
    weight_copy(0).start()
    weight_out[1] = dot_tn(normed[own_normed_rows, other_cols], up_delta[...]).astype(BF16)
    weight_copy(1).start()

    def wait_share(i, carry):
        source = wrapped(t + i, n_tensor)
        share_copy(source, t, source).wait_recv()
        return carry

    lax.fori_loop(1, n_tensor, wait_share, 0)
    total = share_in[0].astype(F32)
    for k in range(1, n_tensor):
        total = total + share_in[k].astype(F32)
    own_group = s * groups + t // 2
    own_half = lax.rem(t, 2)
    share_out[t] = total.astype(BF16)

    def spread_copy(slot, peer, group):
        return pltpu.make_async_remote_copy(
            src_ref=share_out.at[t],
            dst_ref=normed_delta.at[group],
            send_sem=spread_sems.at[0, slot],
            recv_sem=spread_sems.at[1, group],
            device_id=(d, own_half, peer),
            device_id_type=MESH,
        )

    other_copy = pltpu.make_async_remote_copy(
        src_ref=share_out.at[t],
        dst_ref=other_half,
        send_sem=other_sems.at[0],
        recv_sem=other_sems.at[1],
        device_id=(d, 1 - own_half, own_group),
        device_id_type=MESH,
    )
    keeps = own_half == s
    other_here = (own_half != s) & (own_group == t)

    def send_spread(i, carry):
        spread_copy(i, wrapped(t + i, n_tensor), own_group).start()
        return carry

    lax.fori_loop(1, n_tensor, send_spread, 0)

    @pl.when(keeps)
    def _():
        normed_delta[own_group] = share_out[t]

    @pl.when(jnp.logical_not(keeps))
    def _():
        spread_copy(0, t, own_group).start()

    @pl.when(other_here)
    def _():
        other_half[...] = share_out[t]

    @pl.when(jnp.logical_not(other_here))
    def _():
        other_copy.start()

    def wait_z(i, carry):
        source = wrapped(d + i, n_dp)
        z_copy(i, source, source).wait_recv()
        return carry

    lax.fori_loop(1, n_dp, wait_z, 0)
    z_total = dot_z[0]
    for k in range(1, n_dp):
        z_total = z_total + dot_z[k]
    dot_plane[me] = z_total

    def plane_copy(i, source):
        return pltpu.make_async_remote_copy(
            src_ref=dot_plane.at[me],
            dst_ref=dot_plane.at[source],
            send_sem=plane_sems.at[0, i],
            recv_sem=plane_sems.at[1, source],
            device_id=plane_device(i),
            device_id_type=MESH,
        )

    def send_plane(i, carry):
        plane_copy(i, me).start()
        return carry

    lax.fori_loop(1, n_plane, send_plane, 0)

    weight_own[0] = dot_tn(normed[own_normed_rows, own_cols], gate_delta[...])
    weight_own[1] = dot_tn(normed[own_normed_rows, own_cols], up_delta[...])

    def wait_spread(group, carry):
        side = group // groups
        owner = 2 * lax.rem(group, groups) + s

        @pl.when(jnp.logical_not((side == s) & (owner == t)))
        def _():
            spread_copy(0, t, group).wait_recv()

        return carry

    lax.fori_loop(0, n_tensor, wait_spread, 0)

    scale = 1.0 / (features * n_dp)

    def finish(weighted_value, residual_value, rms_value, gain_value, delta_value, dot_value):
        row_scale = rms_value * rms_value * rms_value * dot_value * scale
        return weighted_value + rms_value * gain_value * delta_value - residual_value * row_scale

    def base_block(i, carry):
        block = row_block(i * pair_rows, pair_rows)
        rms_value = rms[block, :]
        base[block, :] = weighted[block, own_cols].astype(F32) + rms_value * gain_row[
            :, own_cols
        ] * jnp.concatenate(
            [normed_delta[2 * i].astype(F32), normed_delta[2 * i + 1].astype(F32)], axis=0
        )
        pull[block, :] = residual[block, own_cols].astype(F32) * (
            rms_value * rms_value * rms_value * scale
        )
        return carry

    lax.fori_loop(0, n_tensor // 2, base_block, 0)

    def wait_plane(i, carry):
        plane_copy(i, wrapped(me + i, n_plane)).wait_recv()
        return carry

    lax.fori_loop(1, n_plane, wait_plane, 0)
    for side in range(2):
        line = dot_plane[side * n_tensor]
        for k in range(1, n_tensor):
            line = line + dot_plane[side * n_tensor + k]
        for b in range(row_products.shape[0] // 128):
            cols = slice(128 * b, 128 * b + 128)
            dot_column[side, cols, :] = jnp.transpose(jnp.broadcast_to(line[:, cols], (128, 128)))

    def finish_block(i, carry):
        block = row_block(i * pair_rows, pair_rows)
        side = i // half_pairs
        local = row_block((i - side * half_pairs) * pair_rows, pair_rows)
        value = base[block, :] - pull[block, :] * dot_column[side, local, :]
        grads[block, :] = value.astype(BF16)
        grad_groups[2 * i] = value[:group_rows].astype(BF16)
        grad_groups[2 * i + 1] = value[group_rows:].astype(BF16)
        return carry

    lax.fori_loop(0, n_tensor // 2, finish_block, 0)
    output_grad[...] = dot_tn(context[...], grads[...]).astype(BF16)
    residual_grad[:, own_cols] = grad_groups[t]

    @pl.when(jnp.logical_not((t // groups == s) & (2 * lax.rem(t, groups) + 1 - s == t)))
    def _():
        other_copy.wait_recv()

    pair = t // 2
    pair_block = row_block(pair * pair_rows, pair_rows)
    pair_side = pair // half_pairs
    pair_local = row_block((pair - pair_side * half_pairs) * pair_rows, pair_rows)

    def own_rows(value):
        return jnp.where(own_half == 0, value[:group_rows], value[group_rows:])

    residual_grad[:, other_cols] = finish(
        own_rows(weighted[pair_block, other_cols].astype(F32)),
        own_rows(residual[pair_block, other_cols].astype(F32)),
        own_rows(rms[pair_block, :]),
        gain_row[:, other_cols],
        other_half[...].astype(F32),
        own_rows(dot_column[pair_side, pair_local, :]),
    ).astype(BF16)

    for index, target in enumerate((gate_grad, up_grad)):
        weight_copy(index).wait_recv()
        target[...] = (weight_own[index] + weight_in[index].astype(F32)).astype(BF16)

    for p in range(PIECES):
        for place in PLACES:
            if goes(place, p):
                sum_copy(place, p).wait_send()
                gather_copy(place, p).wait_send()

    def drain_z(i, carry):
        z_copy(i, wrapped(d + i, n_dp), d).wait_send()
        return carry

    lax.fori_loop(1, n_dp, drain_z, 0)

    def drain_plane(i, carry):
        plane_copy(i, me).wait_send()
        return carry

    lax.fori_loop(1, n_plane, drain_plane, 0)

    def drain_share(i, carry):
        owner = wrapped(t + i, n_tensor)
        share_copy(owner, owner, t).wait_send()
        spread_copy(i, owner, own_group).wait_send()
        return carry

    lax.fori_loop(1, n_tensor, drain_share, 0)

    @pl.when(jnp.logical_not(keeps))
    def _():
        spread_copy(0, t, own_group).wait_send()

    @pl.when(jnp.logical_not(other_here))
    def _():
        other_copy.wait_send()

    for index in range(2):
        weight_copy(index).wait_send()


def hand_on(*refs):
    count = len(refs) // 2
    for source, target in zip(refs[:count], refs[count:]):
        target[...] = source[...]


def shards(
    n_dp,
    n_tensor,
    context,
    residual,
    inverse_rms,
    norm_gain,
    gate_preact,
    up_preact,
    upstream,
    gate_weight,
    up_weight,
    down_weight,
    policy_logprob,
    ref_logprob,
    lengths,
):
    rows, features = residual.shape
    hidden = gate_preact.shape[1]
    half_rows = rows // 2
    groups = n_tensor // 2
    group_rows = half_rows // groups
    tiles = half_rows // 16 * (hidden // 128)
    chunk_tiles = -(-tiles // (n_dp * PIECES)) * PIECES
    ways = len(PLACES)
    padded = -(-half_rows // 128) * 128
    vmem = pl.BlockSpec(memory_space=pltpu.VMEM)
    hbm = pl.BlockSpec(memory_space=pl.ANY)

    def like(array):
        return pltpu.VMEM(array.shape, array.dtype)

    dma = pltpu.SemaphoreType.DMA
    size = (n_dp, n_tensor, rows, hidden, features)
    out_shape = (
            jax.ShapeDtypeStruct((rows // n_tensor, features), BF16),
            jax.ShapeDtypeStruct((context.shape[1], features // 2), BF16),
            jax.ShapeDtypeStruct((features // 2, hidden), BF16),
            jax.ShapeDtypeStruct((features // 2, hidden), BF16),
            jax.ShapeDtypeStruct((hidden, features // 2), BF16),
    )
    grads = pl.pallas_call(
        functools.partial(kernel, size),
        out_shape=out_shape,
        in_specs=[hbm, hbm, hbm, vmem, hbm, hbm, hbm, hbm, hbm, hbm, vmem, vmem, vmem],
        out_specs=(vmem,) * 5,
        scratch_shapes=[
            like(context),
            like(residual),
            like(gate_preact),
            like(up_preact),
            like(upstream),
            like(gate_weight),
            like(up_weight),
            like(down_weight),
            pltpu.VMEM((rows, features), BF16),
            pltpu.VMEM((rows, features), BF16),
            pltpu.VMEM((1, rows), F32),
            pltpu.VMEM((rows, 128), F32),
            pltpu.VMEM((n_dp * chunk_tiles, 16, 128), BF16),
            pltpu.VMEM((ways, chunk_tiles, 16, 128), BF16),
            pltpu.VMEM((ways, chunk_tiles, 16, 128), BF16),
            pltpu.VMEM((n_dp * chunk_tiles, 16, 128), BF16),
            pltpu.VMEM((half_rows, hidden), F32),
            pltpu.VMEM((half_rows, hidden), F32),
            pltpu.VMEM((half_rows, hidden), F32),
            pltpu.VMEM((half_rows, hidden), BF16),
            pltpu.VMEM((half_rows, hidden), BF16),
            pltpu.VMEM((hidden, features // 2), F32),
            pltpu.VMEM((padded, 128), F32),
            pltpu.VMEM((n_tensor, group_rows, 128), BF16),
            pltpu.VMEM((n_tensor, group_rows, 128), BF16),
            pltpu.VMEM((n_tensor, group_rows, 128), BF16),
            pltpu.VMEM((group_rows, 128), BF16),
            pltpu.VMEM((n_dp, 1, padded), F32),
            pltpu.VMEM((2 * n_tensor, 1, padded), F32),
            pltpu.VMEM((2, padded, 128), F32),
            pltpu.VMEM((rows, 128), F32),
            pltpu.VMEM((rows, 128), F32),
            pltpu.VMEM((rows, 128), BF16),
            pltpu.VMEM((n_tensor, group_rows, 128), BF16),
            pltpu.VMEM((2, features // 2, hidden), BF16),
            pltpu.VMEM((2, features // 2, hidden), BF16),
            pltpu.VMEM((2, features // 2, hidden), F32),
            dma((9,)),
            dma((2, ways, PIECES)),
            dma((2, ways, PIECES)),
            dma((2, n_tensor)),
            dma((2, n_tensor)),
            dma((2,)),
            dma((2, n_dp)),
            dma((2, 2 * n_tensor)),
            dma((2, 2)),
        ],
        compiler_params=pltpu.CompilerParams(
            collective_id=0, has_side_effects=True, vmem_limit_bytes=63 * 1024 * 1024
        ),
    )(
        context,
        residual,
        inverse_rms,
        norm_gain.reshape(1, -1),
        gate_preact,
        up_preact,
        upstream,
        gate_weight,
        up_weight,
        down_weight,
        policy_logprob.reshape(1, -1),
        ref_logprob.reshape(1, -1),
        lengths.reshape(1, -1),
    )
    return pl.pallas_call(
        hand_on,
        out_shape=out_shape,
        in_specs=[vmem] * 5,
        out_specs=(vmem,) * 5,
    )(*grads)


def solution(mesh):
    return jax.shard_map(
        functools.partial(shards, mesh.shape["dp"], mesh.shape["tensor"]),
        mesh=mesh,
        in_specs=(
            P(None, "tensor"),
            P(None, "dp"),
            P(),
            P("dp"),
            P(None, "tensor"),
            P(None, "tensor"),
            P(None, "dp"),
            P("dp", "tensor"),
            P("dp", "tensor"),
            P("tensor", "dp"),
            P(),
            P(),
            P(),
        ),
        out_specs=(
            P("tensor", "dp"),
            P("tensor", ("dp", "segment")),
            P(("dp", "segment"), "tensor"),
            P(("dp", "segment"), "tensor"),
            P("tensor", ("dp", "segment")),
        ),
        check_vma=False,
    )
```

```python
import functools
import math

import jax
import jax.numpy as jnp
from jax import lax
from jax.experimental import pallas as pl
from jax.experimental.pallas import tpu as pltpu
from jax.sharding import PartitionSpec as P

POS = 36
LEN = 4096
PIECES = 2
PLACES = (8, -8, 7, -7, 6, -6, 5, -5, 4, -4, 3, -3, 2, -2, 1, -1)
CHAIN = (8, 6, 4, 2, 0)
MESH = pl.DeviceIdType.MESH
BF16 = jnp.bfloat16
F32 = jnp.float32


def wrapped(value, count):
    return lax.rem(value + count, count)


def inward(place):
    below = max(c for c in CHAIN if c < abs(place))
    return below if place > 0 else -below


def goes(place, piece):
    if abs(place) < 8:
        return True
    return (place > 0) == (piece < PIECES // 2)


def feeders(place, piece):
    return [q for q in PLACES if inward(q) == place and goes(q, piece)]


def dot_nt(a, b):
    return lax.dot_general(a, b, (((1,), (1,)), ((), ())), preferred_element_type=F32)


def dot_tn(a, b):
    return lax.dot_general(a, b, (((0,), (0,)), ((), ())), preferred_element_type=F32)


def kernel(
    size,
    context_hbm,
    residual_hbm,
    rms_hbm,
    gain_row,
    gate_hbm,
    up_hbm,
    upstream_hbm,
    gate_weight_hbm,
    up_weight_hbm,
    down_weight_hbm,
    policy_row,
    ref_row,
    lengths_row,
    residual_grad,
    output_grad,
    gate_grad,
    up_grad,
    down_grad,
    context,
    residual,
    gate,
    up,
    upstream,
    gate_weight,
    up_weight,
    down_weight,
    weighted,
    normed,
    rms_row,
    rms,
    partial,
    arrived,
    relayed,
    delta,
    gate_factor,
    up_factor,
    dot_factor,
    gate_delta,
    up_delta,
    down_total,
    row_products,
    share_out,
    share_in,
    normed_delta,
    other_half,
    dot_z,
    dot_plane,
    dot_column,
    base,
    pull,
    grads,
    grad_groups,
    weight_out,
    weight_in,
    weight_own,
    load_sem,
    sum_sems,
    gather_sems,
    share_sems,
    spread_sems,
    other_sems,
    z_sems,
    plane_sems,
    weight_sems,
):
    n_dp, n_tensor, rows, hidden, features = size
    half_rows = rows // 2
    lane_tiles = hidden // 128
    chunk_tiles = partial.shape[0] // n_dp
    piece = chunk_tiles // PIECES
    groups = n_tensor // 2
    group_rows = half_rows // groups
    pair_rows = 2 * group_rows
    half_pairs = half_rows // pair_rows
    n_plane = 2 * n_tensor

    d = lax.axis_index("dp")
    s = lax.axis_index("segment")
    t = lax.axis_index("tensor")
    me = s * n_tensor + t
    row_base = s * half_rows
    own_cols = pl.ds(pl.multiple_of(s * 128, 128), 128)
    other_cols = pl.ds(pl.multiple_of((1 - s) * 128, 128), 128)

    def row_block(start, count):
        return pl.ds(pl.multiple_of(start, 16), count)

    loads = [
        pltpu.make_async_copy(source, target, load_sem.at[index])
        for index, (source, target) in enumerate(
            (
                (upstream_hbm, upstream),
                (down_weight_hbm, down_weight),
                (gate_hbm, gate),
                (up_hbm, up),
                (residual_hbm, residual),
                (gate_weight_hbm, gate_weight),
                (up_weight_hbm, up_weight),
                (context_hbm, context),
                (rms_hbm, rms_row.at[0]),
            )
        )
    ]
    for load in loads:
        load.start()

    barrier = pltpu.get_barrier_semaphore()

    def greet_z(i, carry):
        pl.semaphore_signal(
            barrier, inc=1, device_id=(wrapped(d + i, n_dp), s, t), device_id_type=MESH
        )
        return carry

    def plane_device(i):
        peer = wrapped(me + i, n_plane)
        return (d, peer // n_tensor, lax.rem(peer, n_tensor))

    def greet_plane(i, carry):
        pl.semaphore_signal(barrier, inc=1, device_id=plane_device(i), device_id_type=MESH)
        return carry

    for offset in (1, 2, 3):
        greet_z(offset, 0)
        greet_z(-offset, 0)
    lax.fori_loop(1, n_plane, greet_plane, 0)

    npo = 2.0 * jax.nn.sigmoid(0.1 * (policy_row[...] - ref_row[...]))
    valid = lengths_row[...] - (LEN - POS)
    sequences = npo.shape[1]
    loads[0].wait()

    def weigh(i, carry):
        start = i * 144
        row = lax.broadcasted_iota(jnp.int32, (144, sequences), 0) + start
        offset = row - POS * lax.broadcasted_iota(jnp.int32, (144, sequences), 1)
        keep = (offset >= 0) & (offset < POS) & (offset < valid)
        weight = jnp.sum(jnp.where(keep, npo, 0.0), axis=1, keepdims=True)
        block = row_block(start, 144)
        weighted[block, :] = (upstream[block, :].astype(F32) * weight).astype(BF16)
        return carry

    lax.fori_loop(0, rows // 144, weigh, 0)
    loads[1].wait()

    def first_product(i, carry):
        block = weighted[row_block(row_base + 64 * i, 64), :]
        product = dot_nt(block, down_weight[...])
        for r in range(4):
            for c in range(lane_tiles):
                partial[(4 * i + r) * lane_tiles + c] = product[
                    16 * r : 16 * r + 16, 128 * c : 128 * c + 128
                ].astype(BF16)
        return carry

    lax.fori_loop(0, half_rows // 64, first_product, 0)
    for tile in range(half_rows // 16 * lane_tiles, partial.shape[0]):
        partial[tile] = jnp.zeros((16, 128), BF16)

    def factor_block(i):
        block = row_block(i * 144, 144)
        source = row_block(row_base + i * 144, 144)
        gate_value = gate[source, :].astype(F32)
        up_value = up[source, :].astype(F32)
        squash = jax.nn.sigmoid(gate_value)
        gate_part = up_value * squash * (1.0 + gate_value * (1.0 - squash))
        up_part = gate_value * squash
        gate_factor[block, :] = gate_part
        up_factor[block, :] = up_part
        gained = (residual[source, :].astype(F32) * gain_row[...]).astype(BF16)
        dot_factor[block, :] = gate_part * jnp.dot(
            gained, gate_weight[...], preferred_element_type=F32
        ) + up_part * jnp.dot(gained, up_weight[...], preferred_element_type=F32)

    def hidden_block(i):
        block = row_block(i * 144, 144)
        gate_value = gate[block, :].astype(F32)
        up_value = up[block, :].astype(F32)
        value = (gate_value * jax.nn.sigmoid(gate_value) * up_value).astype(BF16)
        down_total[...] += dot_tn(value, weighted[block, own_cols])

    def norm_block(i):
        block = row_block(i * 128, 128)
        column = jnp.transpose(
            jnp.broadcast_to(rms_row[:, pl.ds(pl.multiple_of(i * 128, 128), 128)], (128, 128))
        )
        rms[block, :] = column
        for c in range(features // 128):
            cols = slice(128 * c, 128 * c + 128)
            normed[block, cols] = (
                residual[block, cols].astype(F32) * column * gain_row[:, cols]
            ).astype(BF16)

    down_total[...] = jnp.zeros(down_total.shape, F32)

    pl.semaphore_wait(barrier, 6 + n_plane - 1)

    def at_z(offset):
        return (wrapped(d + offset, n_dp), s, t)

    def tiles_of(chunk, p):
        return pl.ds(chunk * chunk_tiles + p * piece, piece)

    def sum_copy(place, p):
        chunk = wrapped(d - place, n_dp)
        here = pl.ds(p * piece, piece)
        slot = PLACES.index(place)
        held = relayed.at[slot, here] if feeders(place, p) else partial.at[tiles_of(chunk, p)]
        return pltpu.make_async_remote_copy(
            src_ref=held,
            dst_ref=arrived.at[slot, here],
            send_sem=sum_sems.at[0, slot, p],
            recv_sem=sum_sems.at[1, slot, p],
            device_id=at_z(inward(place) - place),
            device_id_type=MESH,
        )

    def added(place, p):
        here = pl.ds(p * piece, piece)
        value = partial[tiles_of(wrapped(d - place, n_dp), p)].astype(F32)
        for feeder in feeders(place, p):
            sum_copy(feeder, p).wait_recv()
            value = value + arrived[PLACES.index(feeder), here].astype(F32)
        return value.astype(BF16)

    links = [c for c in CHAIN if 0 < c < n_dp // 2]

    def join(number):
        link = (links + [0])[number] if number <= len(links) else None
        for p in range(PIECES):
            for place in PLACES:
                if abs(inward(place)) == link and goes(place, p) and not feeders(place, p):
                    sum_copy(place, p).start()

    join(0)
    join(1)
    for load in loads[2:7]:
        load.wait()
    factor_steps = half_rows // 144
    for number, link in enumerate(links):
        if number < factor_steps:
            factor_block(number)
        for p in range(PIECES):
            for place in (link, -link):
                relayed[PLACES.index(place), pl.ds(p * piece, piece)] = added(place, p)
                sum_copy(place, p).start()
        join(number + 2)
    for number in range(len(links), factor_steps):
        factor_block(number)

    def gather_copy(place, p):
        tiles = tiles_of(wrapped(d - inward(place), n_dp), p)
        slot = PLACES.index(place)
        return pltpu.make_async_remote_copy(
            src_ref=delta.at[tiles],
            dst_ref=delta.at[tiles],
            send_sem=gather_sems.at[0, slot, p],
            recv_sem=gather_sems.at[1, slot, p],
            device_id=at_z(place - inward(place)),
            device_id_type=MESH,
        )

    def gate_block(i, carry):
        block = row_block(i * 16, 16)
        value = jnp.concatenate(
            [delta[i * lane_tiles + c] for c in range(lane_tiles)], axis=1
        ).astype(F32)
        gate_delta[block, :] = (value * gate_factor[block, :]).astype(BF16)
        up_delta[block, :] = (value * up_factor[block, :]).astype(BF16)
        dots = value * dot_factor[block, :]
        row_products[block, :] = sum(
            dots[:, 128 * c : 128 * c + 128] for c in range(lane_tiles)
        )
        return carry


    def share_copy(slot, owner, source):
        return pltpu.make_async_remote_copy(
            src_ref=share_out.at[slot],
            dst_ref=share_in.at[source],
            send_sem=share_sems.at[0, slot],
            recv_sem=share_sems.at[1, source],
            device_id=(d, s, owner),
            device_id_type=MESH,
        )

    def share_block(i, carry):
        block = row_block(i * pair_rows, pair_rows)
        product = dot_nt(gate_delta[block, :], gate_weight[...]) + dot_nt(
            up_delta[block, :], up_weight[...]
        )
        for q in range(2):
            for c in range(2):
                owner = 4 * i + 2 * q + c
                share_out[owner] = product[
                    q * group_rows : (q + 1) * group_rows, 128 * c : 128 * c + 128
                ].astype(BF16)

                @pl.when(owner != t)
                def _():
                    share_copy(owner, owner, t).start()

                @pl.when(owner == t)
                def _():
                    share_in[t] = share_out[t]

        return carry

    pair_tiles = pair_rows // 16

    def token_block(i):
        lax.fori_loop(i * pair_tiles, (i + 1) * pair_tiles, gate_block, 0)
        share_block(i, 0)

    row_products[half_rows:, :] = jnp.zeros((row_products.shape[0] - half_rows, 128), F32)
    here = d // (n_dp // half_pairs)
    lean = lax.rem(d, n_dp // half_pairs)
    early = lean < n_dp // half_pairs // 2
    beside = jnp.where(early, here + half_pairs - 1, here + 1)
    across = jnp.where(early, here + 1, here + half_pairs - 1)
    arrived_places = set()

    def reach(limit):
        for p in range(PIECES):
            for place in PLACES:
                if abs(place) <= limit and goes(place, p) and (place, p) not in arrived_places:
                    arrived_places.add((place, p))
                    gather_copy(place, p).wait_recv()

    for p in range(PIECES):
        delta[tiles_of(d, p)] = added(0, p)
        for place in feeders(0, p):
            gather_copy(place, p).start()
    loads[8].wait()
    norm_block(0)
    hidden_steps = rows // 144
    norm_steps = rows // 128
    links = links[::-1]
    ends = [i * hidden_steps // len(links) for i in range(len(links) + 1)]
    norm_ends = [1 + i * (norm_steps - 1) // len(links) for i in range(len(links) + 1)]
    for number, link in enumerate(links):
        for p in range(PIECES):
            for place in (link, -link):
                arrived_places.add((place, p))
                gather_copy(place, p).wait_recv()
                for fed in feeders(place, p):
                    gather_copy(fed, p).start()
        lax.fori_loop(ends[number], ends[number + 1], lambda i, c: (hidden_block(i), c)[1], 0)
        lax.fori_loop(
            norm_ends[number], norm_ends[number + 1], lambda i, c: (norm_block(i), c)[1], 0
        )
        if link == 4:
            reach(4)
            token_block(here)
        if link == 6:
            reach(6)
            token_block(lax.rem(beside, half_pairs))
    down_grad[...] = down_total[...].astype(BF16)
    loads[7].wait()
    reach(n_dp // 2)
    token_block(lax.rem(here + 2, half_pairs))
    token_block(lax.rem(across, half_pairs))

    def z_copy(slot, peer, source):
        return pltpu.make_async_remote_copy(
            src_ref=dot_z.at[d],
            dst_ref=dot_z.at[source],
            send_sem=z_sems.at[0, slot],
            recv_sem=z_sems.at[1, source],
            device_id=(peer, s, t),
            device_id_type=MESH,
        )

    for b in range(row_products.shape[0] // 128):
        cols = slice(128 * b, 128 * b + 128)
        dot_z[d, :, cols] = jnp.sum(jnp.transpose(row_products[cols, :]), axis=0, keepdims=True)

    def send_z(i, carry):
        z_copy(i, wrapped(d + i, n_dp), d).start()
        return carry

    lax.fori_loop(1, n_dp, send_z, 0)

    own_normed_rows = row_block(row_base, half_rows)
    partner = (d, 1 - s, t)

    def weight_copy(index):
        return pltpu.make_async_remote_copy(
            src_ref=weight_out.at[index],
            dst_ref=weight_in.at[index],
            send_sem=weight_sems.at[0, index],
            recv_sem=weight_sems.at[1, index],
            device_id=partner,
            device_id_type=MESH,
        )

    weight_out[0] = dot_tn(normed[own_normed_rows, other_cols], gate_delta[...]).astype(BF16)
    weight_copy(0).start()
    weight_out[1] = dot_tn(normed[own_normed_rows, other_cols], up_delta[...]).astype(BF16)
    weight_copy(1).start()

    def wait_share(i, carry):
        source = wrapped(t + i, n_tensor)
        share_copy(source, t, source).wait_recv()
        return carry

    lax.fori_loop(1, n_tensor, wait_share, 0)
    total = share_in[0].astype(F32)
    for k in range(1, n_tensor):
        total = total + share_in[k].astype(F32)
    own_group = s * groups + t // 2
    own_half = lax.rem(t, 2)
    share_out[t] = total.astype(BF16)

    def spread_copy(slot, peer, group):
        return pltpu.make_async_remote_copy(
            src_ref=share_out.at[t],
            dst_ref=normed_delta.at[group],
            send_sem=spread_sems.at[0, slot],
            recv_sem=spread_sems.at[1, group],
            device_id=(d, own_half, peer),
            device_id_type=MESH,
        )

    other_copy = pltpu.make_async_remote_copy(
        src_ref=share_out.at[t],
        dst_ref=other_half,
        send_sem=other_sems.at[0],
        recv_sem=other_sems.at[1],
        device_id=(d, 1 - own_half, own_group),
        device_id_type=MESH,
    )
    keeps = own_half == s
    other_here = (own_half != s) & (own_group == t)

    def send_spread(i, carry):
        spread_copy(i, wrapped(t + i, n_tensor), own_group).start()
        return carry

    lax.fori_loop(1, n_tensor, send_spread, 0)

    @pl.when(keeps)
    def _():
        normed_delta[own_group] = share_out[t]

    @pl.when(jnp.logical_not(keeps))
    def _():
        spread_copy(0, t, own_group).start()

    @pl.when(other_here)
    def _():
        other_half[...] = share_out[t]

    @pl.when(jnp.logical_not(other_here))
    def _():
        other_copy.start()

    def wait_z(i, carry):
        source = wrapped(d + i, n_dp)
        z_copy(i, source, source).wait_recv()
        return carry

    lax.fori_loop(1, n_dp, wait_z, 0)
    z_total = dot_z[0]
    for k in range(1, n_dp):
        z_total = z_total + dot_z[k]
    dot_plane[me] = z_total

    def plane_copy(i, source):
        return pltpu.make_async_remote_copy(
            src_ref=dot_plane.at[me],
            dst_ref=dot_plane.at[source],
            send_sem=plane_sems.at[0, i],
            recv_sem=plane_sems.at[1, source],
            device_id=plane_device(i),
            device_id_type=MESH,
        )

    def send_plane(i, carry):
        plane_copy(i, me).start()
        return carry

    lax.fori_loop(1, n_plane, send_plane, 0)

    weight_own[0] = dot_tn(normed[own_normed_rows, own_cols], gate_delta[...])
    weight_own[1] = dot_tn(normed[own_normed_rows, own_cols], up_delta[...])

    def wait_spread(group, carry):
        side = group // groups
        owner = 2 * lax.rem(group, groups) + s

        @pl.when(jnp.logical_not((side == s) & (owner == t)))
        def _():
            spread_copy(0, t, group).wait_recv()

        return carry

    lax.fori_loop(0, n_tensor, wait_spread, 0)

    scale = 1.0 / (features * n_dp)

    def finish(weighted_value, residual_value, rms_value, gain_value, delta_value, dot_value):
        row_scale = rms_value * rms_value * rms_value * dot_value * scale
        return weighted_value + rms_value * gain_value * delta_value - residual_value * row_scale

    def base_block(i, carry):
        block = row_block(i * pair_rows, pair_rows)
        rms_value = rms[block, :]
        base[block, :] = weighted[block, own_cols].astype(F32) + rms_value * gain_row[
            :, own_cols
        ] * jnp.concatenate(
            [normed_delta[2 * i].astype(F32), normed_delta[2 * i + 1].astype(F32)], axis=0
        )
        pull[block, :] = residual[block, own_cols].astype(F32) * (
            rms_value * rms_value * rms_value * scale
        )
        return carry

    lax.fori_loop(0, n_tensor // 2, base_block, 0)

    def wait_plane(i, carry):
        plane_copy(i, wrapped(me + i, n_plane)).wait_recv()
        return carry

    lax.fori_loop(1, n_plane, wait_plane, 0)
    for side in range(2):
        line = dot_plane[side * n_tensor]
        for k in range(1, n_tensor):
            line = line + dot_plane[side * n_tensor + k]
        for b in range(row_products.shape[0] // 128):
            cols = slice(128 * b, 128 * b + 128)
            dot_column[side, cols, :] = jnp.transpose(jnp.broadcast_to(line[:, cols], (128, 128)))

    def finish_block(i, carry):
        block = row_block(i * pair_rows, pair_rows)
        side = i // half_pairs
        local = row_block((i - side * half_pairs) * pair_rows, pair_rows)
        value = base[block, :] - pull[block, :] * dot_column[side, local, :]
        grads[block, :] = value.astype(BF16)
        grad_groups[2 * i] = value[:group_rows].astype(BF16)
        grad_groups[2 * i + 1] = value[group_rows:].astype(BF16)
        return carry

    lax.fori_loop(0, n_tensor // 2, finish_block, 0)
    output_grad[...] = dot_tn(context[...], grads[...]).astype(BF16)
    residual_grad[:, own_cols] = grad_groups[t]

    @pl.when(jnp.logical_not((t // groups == s) & (2 * lax.rem(t, groups) + 1 - s == t)))
    def _():
        other_copy.wait_recv()

    pair = t // 2
    pair_block = row_block(pair * pair_rows, pair_rows)
    pair_side = pair // half_pairs
    pair_local = row_block((pair - pair_side * half_pairs) * pair_rows, pair_rows)

    def own_rows(value):
        return jnp.where(own_half == 0, value[:group_rows], value[group_rows:])

    residual_grad[:, other_cols] = finish(
        own_rows(weighted[pair_block, other_cols].astype(F32)),
        own_rows(residual[pair_block, other_cols].astype(F32)),
        own_rows(rms[pair_block, :]),
        gain_row[:, other_cols],
        other_half[...].astype(F32),
        own_rows(dot_column[pair_side, pair_local, :]),
    ).astype(BF16)

    for index, target in enumerate((gate_grad, up_grad)):
        weight_copy(index).wait_recv()
        target[...] = (weight_own[index] + weight_in[index].astype(F32)).astype(BF16)

    for p in range(PIECES):
        for place in PLACES:
            if goes(place, p):
                sum_copy(place, p).wait_send()
                gather_copy(place, p).wait_send()

    def drain_z(i, carry):
        z_copy(i, wrapped(d + i, n_dp), d).wait_send()
        return carry

    lax.fori_loop(1, n_dp, drain_z, 0)

    def drain_plane(i, carry):
        plane_copy(i, me).wait_send()
        return carry

    lax.fori_loop(1, n_plane, drain_plane, 0)

    def drain_share(i, carry):
        owner = wrapped(t + i, n_tensor)
        share_copy(owner, owner, t).wait_send()
        spread_copy(i, owner, own_group).wait_send()
        return carry

    lax.fori_loop(1, n_tensor, drain_share, 0)

    @pl.when(jnp.logical_not(keeps))
    def _():
        spread_copy(0, t, own_group).wait_send()

    @pl.when(jnp.logical_not(other_here))
    def _():
        other_copy.wait_send()

    for index in range(2):
        weight_copy(index).wait_send()


def hand_on(*refs):
    count = len(refs) // 2
    for source, target in zip(refs[:count], refs[count:]):
        target[...] = source[...]


def shards(
    n_dp,
    n_tensor,
    context,
    residual,
    inverse_rms,
    norm_gain,
    gate_preact,
    up_preact,
    upstream,
    gate_weight,
    up_weight,
    down_weight,
    policy_logprob,
    ref_logprob,
    lengths,
):
    rows, features = residual.shape
    hidden = gate_preact.shape[1]
    half_rows = rows // 2
    groups = n_tensor // 2
    group_rows = half_rows // groups
    tiles = half_rows // 16 * (hidden // 128)
    chunk_tiles = -(-tiles // (n_dp * PIECES)) * PIECES
    ways = len(PLACES)
    padded = -(-half_rows // 128) * 128
    vmem = pl.BlockSpec(memory_space=pltpu.VMEM)
    hbm = pl.BlockSpec(memory_space=pl.ANY)

    def like(array):
        return pltpu.VMEM(array.shape, array.dtype)

    dma = pltpu.SemaphoreType.DMA
    size = (n_dp, n_tensor, rows, hidden, features)
    out_shape = (
            jax.ShapeDtypeStruct((rows // n_tensor, features), BF16),
            jax.ShapeDtypeStruct((context.shape[1], features // 2), BF16),
            jax.ShapeDtypeStruct((features // 2, hidden), BF16),
            jax.ShapeDtypeStruct((features // 2, hidden), BF16),
            jax.ShapeDtypeStruct((hidden, features // 2), BF16),
    )
    grads = pl.pallas_call(
        functools.partial(kernel, size),
        out_shape=out_shape,
        in_specs=[hbm, hbm, hbm, vmem, hbm, hbm, hbm, hbm, hbm, hbm, vmem, vmem, vmem],
        out_specs=(vmem,) * 5,
        scratch_shapes=[
            like(context),
            like(residual),
            like(gate_preact),
            like(up_preact),
            like(upstream),
            like(gate_weight),
            like(up_weight),
            like(down_weight),
            pltpu.VMEM((rows, features), BF16),
            pltpu.VMEM((rows, features), BF16),
            pltpu.VMEM((1, rows), F32),
            pltpu.VMEM((rows, 128), F32),
            pltpu.VMEM((n_dp * chunk_tiles, 16, 128), BF16),
            pltpu.VMEM((ways, chunk_tiles, 16, 128), BF16),
            pltpu.VMEM((ways, chunk_tiles, 16, 128), BF16),
            pltpu.VMEM((n_dp * chunk_tiles, 16, 128), BF16),
            pltpu.VMEM((half_rows, hidden), F32),
            pltpu.VMEM((half_rows, hidden), F32),
            pltpu.VMEM((half_rows, hidden), F32),
            pltpu.VMEM((half_rows, hidden), BF16),
            pltpu.VMEM((half_rows, hidden), BF16),
            pltpu.VMEM((hidden, features // 2), F32),
            pltpu.VMEM((padded, 128), F32),
            pltpu.VMEM((n_tensor, group_rows, 128), BF16),
            pltpu.VMEM((n_tensor, group_rows, 128), BF16),
            pltpu.VMEM((n_tensor, group_rows, 128), BF16),
            pltpu.VMEM((group_rows, 128), BF16),
            pltpu.VMEM((n_dp, 1, padded), F32),
            pltpu.VMEM((2 * n_tensor, 1, padded), F32),
            pltpu.VMEM((2, padded, 128), F32),
            pltpu.VMEM((rows, 128), F32),
            pltpu.VMEM((rows, 128), F32),
            pltpu.VMEM((rows, 128), BF16),
            pltpu.VMEM((n_tensor, group_rows, 128), BF16),
            pltpu.VMEM((2, features // 2, hidden), BF16),
            pltpu.VMEM((2, features // 2, hidden), BF16),
            pltpu.VMEM((2, features // 2, hidden), F32),
            dma((9,)),
            dma((2, ways, PIECES)),
            dma((2, ways, PIECES)),
            dma((2, n_tensor)),
            dma((2, n_tensor)),
            dma((2,)),
            dma((2, n_dp)),
            dma((2, 2 * n_tensor)),
            dma((2, 2)),
        ],
        compiler_params=pltpu.CompilerParams(
            collective_id=0, has_side_effects=True, vmem_limit_bytes=63 * 1024 * 1024
        ),
    )(
        context,
        residual,
        inverse_rms,
        norm_gain.reshape(1, -1),
        gate_preact,
        up_preact,
        upstream,
        gate_weight,
        up_weight,
        down_weight,
        policy_logprob.reshape(1, -1),
        ref_logprob.reshape(1, -1),
        lengths.reshape(1, -1),
    )
    return pl.pallas_call(
        hand_on,
        out_shape=out_shape,
        in_specs=[vmem] * 5,
        out_specs=(vmem,) * 5,
    )(*grads)


def solution(mesh):
    return jax.shard_map(
        functools.partial(shards, mesh.shape["dp"], mesh.shape["tensor"]),
        mesh=mesh,
        in_specs=(
            P(None, "tensor"),
            P(None, "dp"),
            P(),
            P("dp"),
            P(None, "tensor"),
            P(None, "tensor"),
            P(None, "dp"),
            P("dp", "tensor"),
            P("dp", "tensor"),
            P("tensor", "dp"),
            P(),
            P(),
            P(),
        ),
        out_specs=(
            P("tensor", "dp"),
            P("tensor", ("dp", "segment")),
            P(("dp", "segment"), "tensor"),
            P(("dp", "segment"), "tensor"),
            P("tensor", ("dp", "segment")),
        ),
        check_vma=False,
    )
```
